256 devices in a mesh: blk: 64 (over y, x_hi, z), az: 4 (over x_lo, core).
Axes of the slice: x: 4 (x_hi: 2, x_lo: 2; x = x_hi * 2 + x_lo), y: 4, z: 8, core: 2. Of those that a mesh axis runs over, the one named last changes fastest.
Arguments:
- lower_part: float32 [64, 512, 512], P('blk', None, 'az'), may hold values from -0.02 to 0.02
- diag_part: float32 [64, 512, 512], P('blk', None, 'az'), may hold values from -0.02 to 0.02
- upper_part: float32 [64, 512, 512], P('blk', None, 'az'), may hold values from -0.02 to 0.02
- right_side: float32 [64, 512, 512], P('blk', None, 'az'), may hold values from -6 to 6
- extra: float32 [32768, 512], P('blk', 'az'), may hold values from -6 to 6
- owners: int32 [32768, 1], P('blk'), may hold values from 0 to 63; in each aligned block of 512 rows (0 to 511, 512 to 1023, ...) at most 16 rows name the same one
- rows_in: int32 [32768], P('blk'), may hold values from 0 to 511
- counts: int32 [64], P('blk'), may hold values from 384 to 512, as said below
Outputs:
- solution: float32 [64, 512, 512], P('blk', None, 'az')
The draws below stay inside these ranges and needn't reach their ends.
Inputs may be any that keep to these rules, and one draw needn't show every extreme that they name: `owners`: within the 512 entries of one subdomain no block row is named more than 16 times; some subdomain names some block row exactly 16 times. `counts`: A subdomain's entries at positions below its count are live, the others are ignored; some subdomain has all 512 entries live.
All inputs are finite; a program needn't handle non-finite values.
Results may differ from the reference program's by a relative error of at most 0.00013.
Values sent between devices are 32-bit elements; how exact they have to be, the bound alone decides.
A program may use at most 64 MiB of HBM per device.

```python
import math
import jax
import jax.numpy as jnp
import numpy as np
from jax import lax

H = 512
R = 512
E_DEV = 512
ENTRIES = 32768
CAP = 16
LEVELS = 4
N_BLK = 64


def draw_counts(key, part):
    lowest = 3 * E_DEV // 4
    values = jax.random.randint(jax.random.fold_in(key, 11), (N_BLK,), lowest, E_DEV + 1)
    chosen = jax.random.randint(jax.random.fold_in(key, 12), (), 0, N_BLK)
    return jnp.where(jnp.arange(N_BLK, dtype=jnp.int32) == chosen, E_DEV, values).astype(jnp.int32)


def with_ends(values, stream_key, smallest, largest):
    shape = values.shape
    index_at = [jax.random.randint(jax.random.fold_in(stream_key, axis), (), 0, shape[axis]) for axis in range(len(shape))]
    values = values.at[tuple(index_at)].set(smallest)
    longest = shape.index(max(shape))
    index_at[longest] = (index_at[longest] + 1) % shape[longest]
    return values.at[tuple(index_at)].set(largest)


def shard_levels(key, shape, shards, smallest, top_value):
    def one(axis_at, parts):
        heights = jax.random.uniform(jax.random.fold_in(jax.random.fold_in(key, 6), axis_at), (parts,), jnp.float32, smallest / len(shards), top_value / len(shards))
        return jnp.repeat(jnp.exp(heights), shape[axis_at] // parts).reshape((-1,) + (1,) * (len(shape) - axis_at - 1))

    factor_of = one(*shards[0])
    for cut in shards[1:]:
        factor_of = factor_of * one(*cut)
    return factor_of


def assign_block(rng, own, number, rows, count, top, bound, lean):
    order = jax.random.permutation(rng, count)
    crowded, common = portions_of(count, rows * top, bound, lean, True), portions_of(count, rows * top, bound, lean, False)
    places = jnp.arange(count)

    def named(lengths, rotation):
        used = int((lengths > 0).sum())
        fixed = max(1, used // 4)
        moved = fixed + (places - fixed + rotation * (used - fixed)) % max(1, count - fixed)
        return jnp.zeros((count,), jnp.int32).at[order[jnp.where(places < fixed, places, moved)]].set(jnp.asarray(lengths, jnp.int32))

    lengths = jnp.where(number % 4 == 0, named(crowded, number // 4), named(common, number - number // 4 - 1))
    mixed = jax.random.permutation(jax.random.fold_in(own, 3), count)
    donor, taker = mixed[0:count // 2 * 2:2], mixed[1:count // 2 * 2:2]
    margin = jnp.minimum(lengths[donor] - 1, bound - lengths[taker]) // 2
    margin = jnp.where((donor == order[0]) | (taker == order[0]) | (lengths[taker] == 0), 0, jnp.maximum(margin, 0))
    moved = jax.random.randint(jax.random.fold_in(own, 4), (count // 2,), 0, 1 << 20) % (margin + 1)
    lengths = lengths.at[donor].add(-moved).at[taker].add(moved)
    labels = jnp.searchsorted(jnp.cumsum(lengths), jnp.arange(rows * top), side="right").astype(jnp.int32)
    grid = labels.reshape(top, rows).T
    grid = grid[jax.random.permutation(jax.random.fold_in(own, 1), rows)]
    rotation = jax.random.randint(jax.random.fold_in(own, 2), (rows, 1), 0, top)
    return jnp.take_along_axis(grid, (jnp.arange(top)[None, :] + rotation) % top, axis=1)


def portions_of(count, total, reach, skew, full):
    portions = [(1 << 20) // math.isqrt(standing ** skew) + 1 for standing in range(1, count + 1)]
    largest = reach if full else min(reach, max(-(-total // count), total * portions[0] // sum(portions)))
    least = 1 if total - largest >= count - 1 else 0
    given, surplus = [largest] + [least] * (count - 1), total - largest - least * (count - 1)
    while surplus > 0:
        candidates = [i for i in range(1, count) if given[i] < largest] or [i for i in range(1, count) if given[i] < reach]
        mass, remaining = sum([portions[i] for i in candidates]), surplus
        for i in candidates:
            more = min(reach - given[i], max(1, remaining * portions[i] // mass), surplus)
            given[i] = given[i] + more
            surplus = surplus - more
    return np.array(given)


def bell_draw(own_key, extent, width, most, split=(), kind=jnp.bfloat16):
    gain = shard_levels(own_key, extent, split, -0.22, 0.18) if split else 1.0
    result = jax.random.normal(own_key, extent, jnp.float32) * width * gain
    return jnp.minimum(jnp.maximum(result, -most), most).astype(kind)


def setup_inputs(seed: int = 0) -> dict:
    key_list = jax.random.split(jax.random.key(seed), 9)
    lower_part = bell_draw(key_list[0], (N_BLK, H, H), 0.006, 0.02, ((0, 64), (2, 4)), jnp.float32)
    diag_part = bell_draw(key_list[1], (N_BLK, H, H), 0.006, 0.02, ((0, 64), (2, 4)), jnp.float32)
    upper_part = bell_draw(key_list[2], (N_BLK, H, H), 0.006, 0.02, ((0, 64), (2, 4)), jnp.float32)
    right_side = bell_draw(key_list[3], (N_BLK, H, R), 1.0, 6.0, ((0, 64), (2, 4)), jnp.float32)
    extra = bell_draw(key_list[4], (ENTRIES, R), 1.0, 6.0, ((0, 64), (1, 4)), jnp.float32)
    owners_keys = jax.random.split(jax.random.fold_in(key_list[5], 1), ENTRIES // E_DEV)
    owners_turns = jax.random.permutation(jax.random.fold_in(key_list[5], 3), ENTRIES // E_DEV)
    owners = jax.vmap(lambda own, number: assign_block(jax.random.fold_in(key_list[5], 2), own, number, E_DEV, N_BLK, 1, CAP, 1))(owners_keys, owners_turns).reshape((ENTRIES, 1))
    rows_in = with_ends(jax.random.randint(key_list[6], (ENTRIES,), 0, H), jax.random.fold_in(key_list[6], 1), 0, H - 1).astype(jnp.int32)
    counts = draw_counts(jax.random.fold_in(key_list[8], 71), 0)
    return dict(lower_part=lower_part, diag_part=diag_part, upper_part=upper_part, right_side=right_side, extra=extra, owners=owners, rows_in=rows_in, counts=counts)


coupling = 0.42


def product(left, right):
    return jnp.einsum("nij,njk->nik", left.astype(jnp.float32), right.astype(jnp.float32), precision=lax.Precision.HIGHEST)


def inverse_apply(diag_block, values):
    first_pass = 2.0 * values - product(diag_block, values)
    second_pass = 2.0 * values - product(diag_block, first_pass)
    return 2.0 * second_pass - product(diag_block, second_pass)


def reference(lower_part, diag_part, upper_part, right_side, extra, owners, rows_in, counts):
    identity = jnp.eye(H, dtype=jnp.float32)
    lower_block = lower_part - coupling * identity
    upper_block = upper_part - coupling * identity
    diag_block = diag_part + identity
    entry_index = jnp.arange(N_BLK * E_DEV, dtype=jnp.int32)
    live_mask = (entry_index % E_DEV) < jnp.repeat(counts, E_DEV)
    flat_rows = (owners[:, 0] * H + rows_in).astype(jnp.int32)
    added = jnp.where(live_mask[:, None], extra, jnp.float32(0.0))
    right_block = right_side.reshape(N_BLK * H, R).at[flat_rows].add(added).reshape(N_BLK, H, R)
    stride = 1
    for level_index in range(LEVELS):
        stacked = inverse_apply(diag_block, jnp.concatenate([lower_block, upper_block, right_block], axis=2))
        from_lower = jnp.roll(stacked, stride, axis=0)
        from_upper = jnp.roll(stacked, -stride, axis=0)
        got_lower = product(lower_block, from_lower)
        got_upper = product(upper_block, from_upper)
        diag_block = diag_block - got_lower[:, :, H:2 * H] - got_upper[:, :, :H]
        right_block = right_block - got_lower[:, :, 2 * H:] - got_upper[:, :, 2 * H:]
        lower_block = -got_lower[:, :, :H]
        upper_block = -got_upper[:, :, H:2 * H]
        stride = stride * 2
    return inverse_apply(diag_block, right_block)
```

```python
import functools

import jax
import jax.numpy as jnp
from jax import lax
from jax.experimental import pallas as pl
from jax.experimental.pallas import tpu as pltpu
from jax.sharding import PartitionSpec as P

coupling = 0.42
MESH = pl.DeviceIdType.MESH
LEVELS = 4
F32, BF16 = jnp.float32, jnp.bfloat16


def product(left, right):
    return jnp.dot(left, right, precision=lax.Precision.HIGHEST, preferred_element_type=jnp.float32)


def deliver(extra, owners, rows_in, counts, block_order):
    cycle_size = lax.axis_size("blk")
    entries = owners.shape[0]
    slot_count = 2 * entries // cycle_size
    owner_ids = owners[:, 0]
    position = lax.iota(jnp.int32, entries)
    live_mask = position < counts[0]
    earlier_same = (
        (owner_ids[:, None] == owner_ids[None, :])
        & live_mask[None, :]
        & (position[None, :] < position[:, None])
    )
    slot_rank = jnp.sum(earlier_same.astype(jnp.int32), axis=1)
    target = jnp.where(live_mask, owner_ids * slot_count + slot_rank, cycle_size * slot_count)
    local_width = extra.shape[1]
    send_values = (
        jnp.zeros((cycle_size * slot_count, local_width), jnp.float32)
        .at[target]
        .set(extra, mode="drop")
    )
    row_marks = (
        jnp.full((cycle_size * slot_count,), -1.0, jnp.float32)
        .at[target]
        .set(rows_in.astype(jnp.float32), mode="drop")
    )
    got_values, got_marks = (
        lax.all_to_all(
            send_values.reshape(cycle_size, slot_count, local_width),
            "blk",
            split_axis=0,
            concat_axis=0,
            tiled=True,
        ),
        lax.all_to_all(
            row_marks.reshape(cycle_size, slot_count),
            "blk",
            split_axis=0,
            concat_axis=0,
            tiled=True,
        ),
    )
    got_values = got_values.reshape(cycle_size * slot_count, local_width)
    got_marks = got_marks.reshape(cycle_size * slot_count)
    row_grid = lax.broadcasted_iota(jnp.int32, (block_order, cycle_size * slot_count), 0).astype(
        jnp.float32
    )
    onehot = (row_grid == got_marks[None, :]).astype(jnp.float32)
    return product(onehot, got_values)


def halves(x):
    hi = x.astype(BF16)
    return hi, (x - hi.astype(F32)).astype(BF16)


def mm(a, b):
    return jnp.dot(a, b, preferred_element_type=F32)


def kernel(
    l_ref, d_ref, u_ref, b_ref, o_ref,
    gath, blocks, sent, got, dh, dl, luh, lul, vh, vl, xh, xl, w_ref, rh, bcur,
    gs, gr, es, er,
):
    n = d_ref.shape[0]
    c = d_ref.shape[1]
    tile = n // 2
    tiles = [pl.ds(t * tile, tile) for t in range(2)]
    blk = lax.axis_index("blk")
    az = lax.axis_index("az")
    cycle = lax.axis_size("blk")
    mate = (az // 2) * 2 + 1 - az % 2
    across = (az + 2) % 4
    diag = (mate + 2) % 4

    def lower(s):
        return (blk - s + cycle) % cycle

    def upper(s):
        return (blk + s) % cycle

    peers = [(blk, mate), (blk, across)]
    for k in range(LEVELS):
        peers += [(lower(2**k), az), (upper(2**k), az)]
    barrier = pltpu.get_barrier_semaphore()
    for peer in peers:
        pl.semaphore_signal(barrier, inc=1, device_id=peer, device_id_type=MESH)
    pl.semaphore_wait(barrier, len(peers))

    started = []

    def gather_copy(k, m, which, slot, device):
        return pltpu.make_async_remote_copy(
            src_ref=gath.at[k, m, slot], dst_ref=gath.at[k, m, slot],
            send_sem=gs.at[k, m, which], recv_sem=gr.at[k, m, which],
            device_id=device, device_id_type=MESH,
        )

    def gather_start(k, m):
        one = gather_copy(k, m, 0, az, (blk, mate))
        two = gather_copy(k, m, 1, az, (blk, across))
        two.start()
        one.start()
        started.extend([one, two])

    def gather_finish(k, m, into_h, into_l, base):
        def put(slot):
            col = pl.ds(pl.multiple_of(base + slot * c, c), c)
            hi, lo = halves(gath[k, m, slot])
            into_h[:, col] = hi
            into_l[:, col] = lo

        put(az)
        gather_copy(k, m, 0, mate, (blk, mate)).wait_recv()
        put(mate)
        gather_copy(k, m, 1, across, (blk, across)).wait_recv()
        three = gather_copy(k, m, 2, across, (blk, mate))
        three.start()
        started.append(three)
        put(across)
        gather_copy(k, m, 2, diag, (blk, mate)).wait_recv()
        put(diag)

    def send(k, which, slot, target):
        copy = pltpu.make_async_remote_copy(
            src_ref=sent.at[k, slot], dst_ref=got.at[k, which],
            send_sem=es.at[k, which], recv_sem=er.at[k, which],
            device_id=(target, az), device_id_type=MESH,
        )
        copy.start()
        started.append(copy)

    def arrived(k, which):
        pltpu.make_async_remote_copy(
            src_ref=sent.at[k, 0], dst_ref=got.at[k, which],
            send_sem=es.at[k, which], recv_sem=er.at[k, which],
            device_id=(blk, az), device_id_type=MESH,
        ).wait_recv()

    def apply_wide(k):
        for part, m in ((0, 1), (1, 2)):
            col = slice(part * c, (part + 1) * c)
            hi, lo = halves(gath[k, m, az])
            vh[:, col] = hi
            vl[:, col] = lo

        def times(rows, hi, lo):
            return mm(dh[rows, :], hi) + mm(dh[rows, :], lo) + mm(dl[rows, :], hi)

        def base(rows):
            return jnp.concatenate([gath[k, 1, az, rows, :], gath[k, 2, az, rows, :]], axis=1)

        for rows in tiles:
            x = 2.0 * base(rows) - times(rows, vh[...], vl[...])
            xh[rows, :], xl[rows, :] = halves(x)
        for rows in tiles:
            w = 2.0 * base(rows) - times(rows, xh[...], xl[...])
            w_ref[rows, :] = w
            vh[rows, :], vl[rows, :] = halves(w)
        for rows in tiles:
            out = 2.0 * w_ref[rows, :] - times(rows, vh[...], vl[...])
            sent[k, 0, rows, :] = out[:, :c]
            sent[k, 1, rows, :] = out[:, c:]

    def narrow(rows, ah, al, pair):
        both = mm(ah[rows, :], pair)
        return both[:, :c] + both[:, c:] + mm(al[rows, :], pair[:, :c])

    def put_pair(ref, rows, x):
        ref[rows, :c], ref[rows, c:] = halves(x)

    def apply_narrow(v_ref, write):
        put_pair(vh, slice(None), v_ref[...])
        for rows in tiles:
            put_pair(xh, rows, 2.0 * v_ref[rows, :] - narrow(rows, dh, dl, vh[...]))
        for rows in tiles:
            w = 2.0 * v_ref[rows, :] - narrow(rows, dh, dl, xh[...])
            w_ref[rows, :c] = w
            put_pair(vh, rows, w)
        for rows in tiles:
            write(rows, 2.0 * w_ref[rows, :c] - narrow(rows, dh, dl, vh[...]))

    def combined(k, first, second, old, write):
        p = k % 2
        put_pair(rh, slice(0, n), got[k, first])
        put_pair(rh, slice(n, 2 * n), got[k, second])
        for rows in tiles:
            pair = rh[...]
            both = mm(luh[p, rows, :], pair)
            value = both[:, :c] + both[:, c:] + mm(lul[p, rows, :], pair[:, :c])
            write(rows, old[rows, :] - value)

    def single(k, which, side, write):
        p = k % 2
        put_pair(rh, slice(0, n), got[k, which])
        col = slice(side * n, (side + 1) * n)
        for rows in tiles:
            pair = rh[0:n, :]
            both = mm(luh[p, rows, col], pair)
            value = both[:, :c] + both[:, c:] + mm(lul[p, rows, col], pair[:, :c])
            write(rows, -value)

    def store(ref):
        def write(rows, value):
            ref[rows, :] = value

        return write

    eye = (
        lax.broadcasted_iota(jnp.int32, (n, c), 0) == lax.broadcasted_iota(jnp.int32, (n, c), 1) + az * c
    ).astype(F32)
    gath[0, 0, az] = d_ref[...] + eye
    gather_start(0, 0)
    gath[0, 1, az] = l_ref[...] - coupling * eye
    gather_start(0, 1)
    gath[0, 2, az] = u_ref[...] - coupling * eye
    gather_start(0, 2)

    QM, PP, PM, QP, YM, YP = range(6)
    for k in range(LEVELS):
        s = 2**k
        last = k == LEVELS - 1
        gather_finish(k, 0, dh, dl, 0)
        apply_wide(k)
        send(k, QM, 1, upper(s))
        send(k, PP, 0, lower(s))
        if not last:
            send(k, PM, 0, upper(s))
            send(k, QP, 1, lower(s))
        if k == 0:
            bcur[0] = b_ref[...]
        else:
            arrived(k - 1, YM)
            arrived(k - 1, YP)
            combined(k - 1, YM, YP, bcur.at[(k - 1) % 2], store(bcur.at[k % 2]))
        apply_narrow(bcur.at[k % 2], store(sent.at[k, 2]))
        send(k, YM, 2, upper(s))
        send(k, YP, 2, lower(s))
        gather_finish(k, 1, luh.at[k % 2], lul.at[k % 2], 0)
        gather_finish(k, 2, luh.at[k % 2], lul.at[k % 2], n)
        arrived(k, QM)
        arrived(k, PP)
        combined(k, QM, PP, gath.at[k, 0, az], store(gath.at[k + 1, 0, az]))
        gather_start(k + 1, 0)
        if not last:
            arrived(k, PM)
            single(k, PM, 0, store(gath.at[k + 1, 1, az]))
            gather_start(k + 1, 1)
            arrived(k, QP)
            single(k, QP, 1, store(gath.at[k + 1, 2, az]))
            gather_start(k + 1, 2)
    gather_finish(LEVELS, 0, dh, dl, 0)
    arrived(LEVELS - 1, YM)
    arrived(LEVELS - 1, YP)
    combined(LEVELS - 1, YM, YP, bcur.at[(LEVELS - 1) % 2], store(bcur.at[LEVELS % 2]))
    apply_narrow(bcur.at[LEVELS % 2], store(o_ref))
    for copy in started:
        copy.wait_send()


def on_device(lower_part, diag_part, upper_part, right_side, extra, owners, rows_in, counts):
    n, c = diag_part.shape[1:]
    right_block = right_side[0] + deliver(extra, owners, rows_in, counts, n)
    vmem = pl.BlockSpec(memory_space=pltpu.VMEM)
    out = pl.pallas_call(
        kernel,
        name="levels",
        out_shape=jax.ShapeDtypeStruct((n, c), F32),
        in_specs=[vmem] * 4,
        out_specs=vmem,
        scratch_shapes=[
            pltpu.VMEM((LEVELS + 1, 3, 4, n, c), F32),
            pltpu.VMEM((8, 128), F32),
            pltpu.VMEM((LEVELS, 3, n, c), F32),
            pltpu.VMEM((LEVELS, 6, n, c), F32),
            pltpu.VMEM((n, n), BF16),
            pltpu.VMEM((n, n), BF16),
            pltpu.VMEM((2, n, 2 * n), BF16),
            pltpu.VMEM((2, n, 2 * n), BF16),
            pltpu.VMEM((n, 2 * c), BF16),
            pltpu.VMEM((n, 2 * c), BF16),
            pltpu.VMEM((n, 2 * c), BF16),
            pltpu.VMEM((n, 2 * c), BF16),
            pltpu.VMEM((n, 2 * c), F32),
            pltpu.VMEM((2 * n, 2 * c), BF16),
            pltpu.VMEM((2, n, c), F32),
            pltpu.SemaphoreType.DMA((LEVELS + 1, 3, 3)),
            pltpu.SemaphoreType.DMA((LEVELS + 1, 3, 3)),
            pltpu.SemaphoreType.DMA((LEVELS, 6)),
            pltpu.SemaphoreType.DMA((LEVELS, 6)),
        ],
        compiler_params=pltpu.CompilerParams(
            collective_id=0, has_side_effects=True, vmem_limit_bytes=56 * 2**20
        ),
    )(lower_part[0], diag_part[0], upper_part[0], right_block)
    return out[None]


def solution(mesh):
    placed = (
        P("blk", None, "az"),
        P("blk", None, "az"),
        P("blk", None, "az"),
        P("blk", None, "az"),
        P("blk", "az"),
        P("blk", None),
        P("blk"),
        P("blk"),
    )
    return jax.shard_map(
        on_device, mesh=mesh, in_specs=placed, out_specs=P("blk", None, "az"), check_vma=False
    )
```

```python
import functools

import jax
import jax.numpy as jnp
from jax import lax
from jax.experimental import pallas as pl
from jax.experimental.pallas import tpu as pltpu
from jax.sharding import PartitionSpec as P

coupling = 0.42
MESH = pl.DeviceIdType.MESH
LEVELS = 4
RING = 8
F32, BF16 = jnp.float32, jnp.bfloat16


def halves(x):
    hi = x.astype(BF16)
    return hi, (x - hi.astype(F32)).astype(BF16)


def mm(a, b):
    return jnp.dot(a, b, preferred_element_type=F32)


def kernel(
    l_ref, d_ref, u_ref, b_ref, x_ref, own_ref, row_ref, cnt_ref, o_ref,
    gath, sent, got, dh, dl, luh, lul, vh, vl, xh, xl, w_ref, rh, bcur,
    out_v, out_m, in_v, in_m, swap, gs, gr, es, er, ps, ws, wr,
):
    n = d_ref.shape[0]
    c = d_ref.shape[1]
    tile = n // 2
    tiles = [pl.ds(t * tile, tile) for t in range(2)]
    blk = lax.axis_index("blk")
    az = lax.axis_index("az")
    cycle = lax.axis_size("blk")
    mate = (az // 2) * 2 + 1 - az % 2
    across = (az + 2) % 4
    odd = (blk // RING) % 2
    col = (az + 2 * odd) % 4

    def lower(s):
        return (blk - s + cycle) % cycle

    def upper(s):
        return (blk + s) % cycle

    def at(row):
        return (row, (col + 2 * ((row // RING) % 2)) % 4)

    entries = x_ref.shape[0]
    slots = out_v.shape[0] // cycle
    barrier = pltpu.get_barrier_semaphore()
    pl.semaphore_signal(barrier, inc=1, device_id=(blk, mate), device_id_type=MESH)
    pl.semaphore_signal(barrier, inc=1, device_id=(blk, across), device_id_type=MESH)

    @pl.loop(1, cycle)
    def _(step):
        to = upper(step)
        pl.semaphore_signal(barrier, inc=1, device_id=(to, az), device_id_type=MESH)
        pl.semaphore_signal(barrier, inc=1, device_id=(to, (az + 2) % 4), device_id_type=MESH)

    started = []

    def gather_copy(k, m, which, slot, device):
        return pltpu.make_async_remote_copy(
            src_ref=gath.at[k, m, slot], dst_ref=gath.at[k, m, slot],
            send_sem=gs.at[k, m, which], recv_sem=gr.at[k, m, which],
            device_id=device, device_id_type=MESH,
        )

    def gather_start(k, m):
        mine = az if k == 0 else col
        one = gather_copy(k, m, 0, mine, (blk, mate))
        two = gather_copy(k, m, 1, mine, (blk, across))
        two.start()
        one.start()
        started.extend([one, two])

    def gather_finish(k, m, into_h, into_l, base):
        mine = az if k == 0 else col
        beside = (mine // 2) * 2 + 1 - mine % 2

        def put(slot):
            where = pl.ds(pl.multiple_of(base + slot * c, c), c)
            hi, lo = halves(gath[k, m, slot])
            into_h[:, where] = hi
            into_l[:, where] = lo

        put(mine)
        gather_copy(k, m, 0, beside, (blk, mate)).wait_recv()
        put(beside)
        gather_copy(k, m, 1, (mine + 2) % 4, (blk, across)).wait_recv()
        three = gather_copy(k, m, 2, (mine + 2) % 4, (blk, mate))
        three.start()
        started.append(three)
        put((mine + 2) % 4)
        gather_copy(k, m, 2, (beside + 2) % 4, (blk, mate)).wait_recv()
        put((beside + 2) % 4)

    def swap_copy(which, src):
        return pltpu.make_async_remote_copy(
            src_ref=src, dst_ref=swap.at[which, 1], send_sem=ws.at[which], recv_sem=wr.at[which],
            device_id=(blk, across), device_id_type=MESH,
        )

    def swap_start(which, src):
        swap[which, 0] = src[...]

        @pl.when(odd == 1)
        def _():
            swap_copy(which, swap.at[which, 0]).start()

    def swap_finish(which):
        @pl.when(odd == 1)
        def _():
            swap_copy(which, swap.at[which, 0]).wait()

    def send(k, which, slot, target):
        copy = pltpu.make_async_remote_copy(
            src_ref=sent.at[k, slot], dst_ref=got.at[k, which],
            send_sem=es.at[k, slot, which // 3], recv_sem=er.at[k, which],
            device_id=target, device_id_type=MESH,
        )
        copy.start()
        started.append(copy)
        return copy

    def arrived(k, which):
        pltpu.make_async_remote_copy(
            src_ref=sent.at[k, 0], dst_ref=got.at[k, which],
            send_sem=er.at[k, which], recv_sem=er.at[k, which],
            device_id=(blk, az), device_id_type=MESH,
        ).wait_recv()

    half = (blk % RING) // (RING // 2)
    near = (blk // RING) * RING + (blk + RING // 2) % RING
    far = (blk + RING * (1 - 2 * half) + cycle) % cycle

    def send_shared(k, slot):
        copy = pltpu.make_async_remote_copy(
            src_ref=sent.at[k, slot], dst_ref=got.at[k, half * 3 + slot],
            send_sem=es.at[k, slot, 0], recv_sem=er.at[k, half * 3 + slot],
            device_id=at(near), device_id_type=MESH,
        )
        copy.start()
        started.append(copy)

    def pass_on(k, slot):
        direct = (1 - half) * 3 + slot
        arrived(k, direct)
        copy = pltpu.make_async_remote_copy(
            src_ref=got.at[k, direct], dst_ref=got.at[k, half * 3 + slot],
            send_sem=es.at[k, slot, 1], recv_sem=er.at[k, half * 3 + slot],
            device_id=at(far), device_id_type=MESH,
        )
        copy.start()
        started.append(copy)

    def arrived_shared(k, slot):
        arrived(k, half * 3 + slot)

    def apply_wide(k):
        for part, m in ((0, 1), (1, 2)):
            hi, lo = halves(gath[k, m, col])
            vh[:, part * c : (part + 1) * c] = hi
            vl[:, part * c : (part + 1) * c] = lo

        def times(rows, hi, lo):
            return mm(dh[rows, :], hi) + mm(dh[rows, :], lo) + mm(dl[rows, :], hi)

        def base(rows):
            return jnp.concatenate([gath[k, 1, col, rows, :], gath[k, 2, col, rows, :]], axis=1)

        for rows in tiles:
            x = 2.0 * base(rows) - times(rows, vh[...], vl[...])
            xh[rows, :], xl[rows, :] = halves(x)
        for rows in tiles:
            w = 2.0 * base(rows) - times(rows, xh[...], xl[...])
            w_ref[rows, :] = w
            vh[rows, :], vl[rows, :] = halves(w)
        for rows in tiles:
            out = 2.0 * w_ref[rows, :] - times(rows, vh[...], vl[...])
            sent[k, 0, rows, :] = out[:, :c]
            sent[k, 1, rows, :] = out[:, c:]

    def narrow(rows, ah, al, pair):
        both = mm(ah[rows, :], pair)
        return both[:, :c] + both[:, c:] + mm(al[rows, :], pair[:, :c])

    def put_pair(ref, rows, x):
        ref[rows, :c], ref[rows, c:] = halves(x)

    def apply_narrow(v_ref, write):
        put_pair(vh, slice(None), v_ref[...])
        for rows in tiles:
            put_pair(xh, rows, 2.0 * v_ref[rows, :] - narrow(rows, dh, dl, vh[...]))
        for rows in tiles:
            w = 2.0 * v_ref[rows, :] - narrow(rows, dh, dl, xh[...])
            w_ref[rows, :c] = w
            put_pair(vh, rows, w)
        for rows in tiles:
            write(rows, 2.0 * w_ref[rows, :c] - narrow(rows, dh, dl, vh[...]))

    def combined(k, first, second, old, write):
        p = k % 2
        put_pair(rh, slice(0, n), got[k, first])
        put_pair(rh, slice(n, 2 * n), got[k, second])
        for rows in tiles:
            pair = rh[...]
            both = mm(luh[p, rows, :], pair)
            value = both[:, :c] + both[:, c:] + mm(lul[p, rows, :], pair[:, :c])
            write(rows, old[rows, :] - value)

    def single(k, which, side, write):
        p = k % 2
        put_pair(rh, slice(0, n), got[k, which])
        cols = slice(side * n, (side + 1) * n)
        for rows in tiles:
            pair = rh[0:n, :]
            both = mm(luh[p, rows, cols], pair)
            value = both[:, :c] + both[:, c:] + mm(lul[p, rows, cols], pair[:, :c])
            write(rows, -value)

    def store(ref):
        def write(rows, value):
            ref[rows, :] = value

        return write

    def pack():
        live = lax.broadcasted_iota(jnp.int32, (1, entries), 1) < cnt_ref[...]
        owner = jnp.where(live, own_ref[...], -1)
        named = jnp.where(lax.broadcasted_iota(jnp.int32, (cycle, entries), 0) == owner, 1.0, 0.0)
        earlier = jnp.where(
            lax.broadcasted_iota(jnp.int32, (entries, entries), 0)
            < lax.broadcasted_iota(jnp.int32, (entries, entries), 1), 1.0, 0.0
        ).astype(BF16)
        before = mm(named.astype(BF16), earlier)
        rank = jnp.sum(named * before, axis=0, keepdims=True).astype(jnp.int32)
        target = jnp.where(live, owner * slots + rank, -1)
        row = row_ref[...]
        place = lax.broadcasted_iota(jnp.int32, (128, entries), 0)
        marks = jnp.where(place == rank, row // slots, jnp.where(place == rank + slots, row % slots, 0))
        out_m[...] = lax.dot_general(
            named.astype(BF16), marks.astype(F32).astype(BF16), (((1,), (1,)), ((), ())),
            preferred_element_type=F32,
        )[:, None, :]
        put_pair(vh, slice(None), x_ref[...])
        part = 256
        for t in range(out_v.shape[0] // part):
            pick = jnp.where(
                lax.broadcasted_iota(jnp.int32, (part, entries), 0) + t * part == target, 1.0, 0.0
            ).astype(BF16)
            both = mm(pick, vh[...])
            out_v[t * part : (t + 1) * part, :] = both[:, :c] + both[:, c:]

    def block_of(ref, index):
        return ref.at[pl.ds(pl.multiple_of(index * slots, slots), slots), :]

    def deliver():
        pltpu.make_async_copy(out_m.at[blk], in_m.at[blk], ps.at[3]).start()

        @pl.when(odd == 0)
        def _():
            pltpu.make_async_copy(block_of(out_v, blk), block_of(in_v, blk), ps.at[1]).start()

        @pl.when(odd == 1)
        def _():
            pltpu.make_async_remote_copy(
                src_ref=block_of(out_v, blk), dst_ref=block_of(in_v, blk), send_sem=ps.at[4], recv_sem=ps.at[1],
                device_id=(blk, across), device_id_type=MESH,
            ).start()

        @pl.loop(1, cycle)
        def _(step):
            to = upper(step)
            pltpu.make_async_remote_copy(
                src_ref=out_m.at[to], dst_ref=in_m.at[blk], send_sem=ps.at[2], recv_sem=ps.at[3],
                device_id=(to, (az + 2 * ((to // RING) % 2)) % 4), device_id_type=MESH,
            ).start()
            pltpu.make_async_remote_copy(
                src_ref=block_of(out_v, to), dst_ref=block_of(in_v, blk), send_sem=ps.at[0], recv_sem=ps.at[1],
                device_id=(to, (az + 2 * ((to // RING) % 2)) % 4), device_id_type=MESH,
            ).start()

    def unpack():
        pltpu.make_async_copy(in_m, in_m, ps.at[3]).wait()
        pltpu.make_async_copy(in_v, in_v, ps.at[1]).wait()
        total = in_v.shape[0]
        lane = lax.broadcasted_iota(jnp.int32, (128, total), 0)
        slot = lax.broadcasted_iota(jnp.int32, (128, total), 1) % slots
        spread = jnp.where(slot == lane, float(slots), jnp.where(slot + slots == lane, 1.0, 0.0))
        wide = mm(in_m[:, 0, :].astype(BF16), spread.astype(BF16))
        mine = lax.broadcasted_iota(jnp.int32, (cycle, total), 1) // slots == lax.broadcasted_iota(
            jnp.int32, (cycle, total), 0
        )
        mark = jnp.sum(jnp.where(mine, wide, 0.0), axis=0, keepdims=True).astype(jnp.int32)
        put_pair(rh, slice(None), in_v[...])
        for rows in tiles:
            pick = jnp.where(
                lax.broadcasted_iota(jnp.int32, (tile, total), 0) + rows.start == mark, 1.0, 0.0
            ).astype(BF16)
            both = mm(pick, rh[...])
            bcur[0, rows, :] = swap[0, odd, rows, :] + both[:, :c] + both[:, c:]

    eye = (
        lax.broadcasted_iota(jnp.int32, (n, c), 0) == lax.broadcasted_iota(jnp.int32, (n, c), 1) + az * c
    ).astype(F32)
    gath[0, 0, az] = d_ref[...] + eye
    gath[0, 1, az] = l_ref[...] - coupling * eye
    gath[0, 2, az] = u_ref[...] - coupling * eye
    pack()
    pl.semaphore_wait(barrier, 2 * cycle)
    for m in range(3):
        gather_start(0, m)

    PM, QM, YM, PP, QP, YP = range(6)
    rhs = []

    def right_side(k):
        s = 2**k
        last = k == LEVELS - 1
        shared = s == RING // 2
        if k == 0:
            swap_finish(0)
            unpack()
        else:
            if s == RING:
                arrived_shared(k - 1, 2)
            else:
                arrived(k - 1, YM)
                arrived(k - 1, YP)
            combined(k - 1, YM, YP, bcur.at[(k - 1) % 2], store(bcur.at[k % 2]))
        if last:
            swap_start(1, bcur.at[k % 2])
        apply_narrow(bcur.at[k % 2], store(sent.at[k, 2]))
        if shared:
            send_shared(k, 2)
        else:
            rhs[:] = [
                send(k, YM, 2, (upper(s), col) if last else at(upper(s))),
                send(k, YP, 2, (lower(s), col) if last else at(lower(s))),
            ]

    for k in range(LEVELS):
        s = 2**k
        last = k == LEVELS - 1
        shared = s == RING // 2
        gather_finish(k, 0, dh, dl, 0)
        if s == RING:
            pass_on(k - 1, 2)
        if k == 0:
            gather_finish(k, 1, luh.at[k % 2], lul.at[k % 2], 0)
            apply_narrow(gath.at[k, 1, col], store(sent.at[k, 0]))
            send(k, PP, 0, at(lower(s)))
            send(k, PM, 0, at(upper(s)))
            swap_start(0, b_ref)
            deliver()
            gather_finish(k, 2, luh.at[k % 2], lul.at[k % 2], n)
            apply_narrow(gath.at[k, 2, col], store(sent.at[k, 1]))
            send(k, QM, 1, at(upper(s)))
            send(k, QP, 1, at(lower(s)))
        else:
            apply_wide(k)
        if k == 0:
            pass
        elif shared:
            for copy in rhs:
                copy.wait_send()
            started[:] = [copy for copy in started if not any(copy is other for other in rhs)]
            send_shared(k, half)
            send_shared(k, 1 - half)
        else:
            send(k, QM, 1, at(upper(s)))
            send(k, PP, 0, at(lower(s)))
            if not last:
                send(k, PM, 0, at(upper(s)))
                send(k, QP, 1, at(lower(s)))
        if k > 0:
            right_side(k)
        if k > 0:
            gather_finish(k, 1, luh.at[k % 2], lul.at[k % 2], 0)
            gather_finish(k, 2, luh.at[k % 2], lul.at[k % 2], n)
        if shared:
            pass_on(k, 1 - half)
            pass_on(k, half)
            arrived_shared(k, 1 - half)
            arrived_shared(k, half)
        else:
            arrived(k, QM)
            arrived(k, PP)
        combined(k, QM, PP, gath.at[k, 0, col], store(gath.at[k + 1, 0, col]))
        gather_start(k + 1, 0)
        if not last:
            if not shared:
                arrived(k, PM)
            single(k, PM, 0, store(gath.at[k + 1, 1, col]))
            gather_start(k + 1, 1)
            if not shared:
                arrived(k, QP)
            single(k, QP, 1, store(gath.at[k + 1, 2, col]))
            gather_start(k + 1, 2)
        if k == 0:
            right_side(k)
    gather_finish(LEVELS, 0, dh, dl, 0)
    arrived(LEVELS - 1, YM)
    arrived(LEVELS - 1, YP)
    swap_finish(1)
    combined(LEVELS - 1, YM, YP, swap.at[1, odd], store(bcur.at[LEVELS % 2]))
    apply_narrow(bcur.at[LEVELS % 2], store(o_ref))
    for copy in started:
        copy.wait_send()
    rest = pl.ds(0, (cycle - 1) * slots)
    pltpu.make_async_copy(out_v.at[rest, :], out_v.at[rest, :], ps.at[0]).wait()

    @pl.when(odd == 1)
    def _():
        pltpu.make_async_copy(block_of(out_v, blk), block_of(in_v, blk), ps.at[4]).wait()

    rest = pl.ds(0, cycle - 1)
    pltpu.make_async_copy(out_m.at[rest], out_m.at[rest], ps.at[2]).wait()


def on_device(lower_part, diag_part, upper_part, right_side, extra, owners, rows_in, counts):
    n, c = diag_part.shape[1:]
    entries = extra.shape[0]
    cycle = lax.axis_size("blk")
    slots = 2 * entries // cycle
    vmem = pl.BlockSpec(memory_space=pltpu.VMEM)
    out = pl.pallas_call(
        kernel,
        name="levels",
        out_shape=jax.ShapeDtypeStruct((n, c), F32),
        in_specs=[vmem] * 8,
        out_specs=vmem,
        scratch_shapes=[
            pltpu.VMEM((LEVELS + 1, 3, 4, n, c), F32),
            pltpu.VMEM((LEVELS, 3, n, c), F32),
            pltpu.VMEM((LEVELS, 6, n, c), F32),
            pltpu.VMEM((n, n), BF16),
            pltpu.VMEM((n, n), BF16),
            pltpu.VMEM((2, n, 2 * n), BF16),
            pltpu.VMEM((2, n, 2 * n), BF16),
            pltpu.VMEM((n, 2 * c), BF16),
            pltpu.VMEM((n, 2 * c), BF16),
            pltpu.VMEM((n, 2 * c), BF16),
            pltpu.VMEM((n, 2 * c), BF16),
            pltpu.VMEM((n, 2 * c), F32),
            pltpu.VMEM((2 * n, 2 * c), BF16),
            pltpu.VMEM((2, n, c), F32),
            pltpu.VMEM((cycle * slots, c), F32),
            pltpu.VMEM((cycle, 1, 128), F32),
            pltpu.VMEM((cycle * slots, c), F32),
            pltpu.VMEM((cycle, 1, 128), F32),
            pltpu.VMEM((2, 2, n, c), F32),
            pltpu.SemaphoreType.DMA((LEVELS + 1, 3, 3)),
            pltpu.SemaphoreType.DMA((LEVELS + 1, 3, 3)),
            pltpu.SemaphoreType.DMA((LEVELS, 3, 2)),
            pltpu.SemaphoreType.DMA((LEVELS, 6)),
            pltpu.SemaphoreType.DMA((5,)),
            pltpu.SemaphoreType.DMA((2,)),
            pltpu.SemaphoreType.DMA((2,)),
        ],
        compiler_params=pltpu.CompilerParams(
            collective_id=0, has_side_effects=True, vmem_limit_bytes=56 * 2**20
        ),
    )(lower_part[0], diag_part[0], upper_part[0], right_side[0], extra,
      owners.reshape(1, entries), rows_in.reshape(1, entries), counts.reshape(1, 1))
    return out[None]


def solution(mesh):
    placed = (
        P("blk", None, "az"),
        P("blk", None, "az"),
        P("blk", None, "az"),
        P("blk", None, "az"),
        P("blk", "az"),
        P("blk", None),
        P("blk"),
        P("blk"),
    )
    return jax.shard_map(
        on_device, mesh=mesh, in_specs=placed, out_specs=P("blk", None, "az"), check_vma=False
    )
```

```python
import functools

import jax
import jax.numpy as jnp
from jax import lax
from jax.experimental import pallas as pl
from jax.experimental.pallas import tpu as pltpu
from jax.sharding import PartitionSpec as P

coupling = 0.42
MESH = pl.DeviceIdType.MESH
LEVELS = 4
RING = 8
F32, BF16 = jnp.float32, jnp.bfloat16


def halves(x):
    hi = x.astype(BF16)
    return hi, (x - hi.astype(F32)).astype(BF16)


def mm(a, b):
    return jnp.dot(a, b, preferred_element_type=F32)


def kernel(
    l_ref, d_ref, u_ref, b_ref, x_ref, own_ref, row_ref, cnt_ref, o_ref,
    gath, sent, got, dh, dl, luh, lul, vh, vl, xh, xl, w_ref, rh, bcur,
    out_v, out_m, in_v, in_m, swap, gs, gr, es, er, ps, ws, wr,
):
    n = d_ref.shape[0]
    c = d_ref.shape[1]
    tile = n // 2
    tiles = [pl.ds(t * tile, tile) for t in range(2)]
    blk = lax.axis_index("blk")
    az = lax.axis_index("az")
    cycle = lax.axis_size("blk")
    mate = (az // 2) * 2 + 1 - az % 2
    across = (az + 2) % 4
    odd = (blk // RING) % 2
    col = (az + 2 * odd) % 4

    def lower(s):
        return (blk - s + cycle) % cycle

    def upper(s):
        return (blk + s) % cycle

    def at(row):
        return (row, (col + 2 * ((row // RING) % 2)) % 4)

    entries = x_ref.shape[0]
    slots = out_v.shape[0] // cycle
    barrier = pltpu.get_barrier_semaphore()
    pl.semaphore_signal(barrier, inc=1, device_id=(blk, mate), device_id_type=MESH)
    pl.semaphore_signal(barrier, inc=1, device_id=(blk, across), device_id_type=MESH)

    @pl.loop(1, cycle)
    def _(step):
        to = upper(step)
        pl.semaphore_signal(barrier, inc=1, device_id=(to, az), device_id_type=MESH)
        pl.semaphore_signal(barrier, inc=1, device_id=(to, (az + 2) % 4), device_id_type=MESH)

    started = []

    def gather_copy(k, m, which, slot, device):
        return pltpu.make_async_remote_copy(
            src_ref=gath.at[k, m, slot], dst_ref=gath.at[k, m, slot],
            send_sem=gs.at[k, m, which], recv_sem=gr.at[k, m, which],
            device_id=device, device_id_type=MESH,
        )

    def gather_start(k, m):
        mine = az if k == 0 else col
        one = gather_copy(k, m, 0, mine, (blk, mate))
        two = gather_copy(k, m, 1, mine, (blk, across))
        two.start()
        one.start()
        started.extend([one, two])

    def gather_finish(k, m, into_h, into_l, base, between=None):
        mine = az if k == 0 else col
        beside = (mine // 2) * 2 + 1 - mine % 2

        def put(slot):
            where = pl.ds(pl.multiple_of(base + slot * c, c), c)
            hi, lo = halves(gath[k, m, slot])
            into_h[:, where] = hi
            into_l[:, where] = lo

        put(mine)
        gather_copy(k, m, 0, beside, (blk, mate)).wait_recv()
        put(beside)
        if between is not None:
            between()
        gather_copy(k, m, 1, (mine + 2) % 4, (blk, across)).wait_recv()
        three = gather_copy(k, m, 2, (mine + 2) % 4, (blk, mate))
        three.start()
        started.append(three)
        put((mine + 2) % 4)
        gather_copy(k, m, 2, (beside + 2) % 4, (blk, mate)).wait_recv()
        put((beside + 2) % 4)

    def swap_copy(which, src):
        return pltpu.make_async_remote_copy(
            src_ref=src, dst_ref=swap.at[which, 1], send_sem=ws.at[which], recv_sem=wr.at[which],
            device_id=(blk, across), device_id_type=MESH,
        )

    def swap_start(which, src):
        swap[which, 0] = src[...]

        @pl.when(odd == 1)
        def _():
            swap_copy(which, swap.at[which, 0]).start()

    def swap_finish(which):
        @pl.when(odd == 1)
        def _():
            swap_copy(which, swap.at[which, 0]).wait()

    def send(k, which, slot, target):
        copy = pltpu.make_async_remote_copy(
            src_ref=sent.at[k, slot], dst_ref=got.at[k, which],
            send_sem=es.at[k, slot, which // 3], recv_sem=er.at[k, which],
            device_id=target, device_id_type=MESH,
        )
        copy.start()
        started.append(copy)
        return copy

    def arrived(k, which):
        pltpu.make_async_remote_copy(
            src_ref=sent.at[k, 0], dst_ref=got.at[k, which],
            send_sem=er.at[k, which], recv_sem=er.at[k, which],
            device_id=(blk, az), device_id_type=MESH,
        ).wait_recv()

    half = (blk % RING) // (RING // 2)
    near = (blk // RING) * RING + (blk + RING // 2) % RING
    far = (blk + RING * (1 - 2 * half) + cycle) % cycle

    def send_shared(k, slot):
        copy = pltpu.make_async_remote_copy(
            src_ref=sent.at[k, slot], dst_ref=got.at[k, half * 3 + slot],
            send_sem=es.at[k, slot, 0], recv_sem=er.at[k, half * 3 + slot],
            device_id=at(near), device_id_type=MESH,
        )
        copy.start()
        started.append(copy)

    def pass_on(k, slot):
        direct = (1 - half) * 3 + slot
        arrived(k, direct)
        copy = pltpu.make_async_remote_copy(
            src_ref=got.at[k, direct], dst_ref=got.at[k, half * 3 + slot],
            send_sem=es.at[k, slot, 1], recv_sem=er.at[k, half * 3 + slot],
            device_id=at(far), device_id_type=MESH,
        )
        copy.start()
        started.append(copy)

    def send_last(k):
        copy = pltpu.make_async_remote_copy(
            src_ref=sent.at[k, 2], dst_ref=got.at[k, 2 + 3 * odd],
            send_sem=es.at[k, 2, 0], recv_sem=er.at[k, 2 + 3 * odd],
            device_id=((blk + RING * (1 - 2 * odd) + cycle) % cycle, col), device_id_type=MESH,
        )
        copy.start()
        started.append(copy)

    def pass_last(k):
        direct = 2 + 3 * (1 - odd)
        arrived(k, direct)
        copy = pltpu.make_async_remote_copy(
            src_ref=got.at[k, direct], dst_ref=got.at[k, 2 + 3 * odd],
            send_sem=es.at[k, 2, 1], recv_sem=er.at[k, 2 + 3 * odd],
            device_id=((blk + 2 * RING * (1 - 2 * odd) + cycle) % cycle, az), device_id_type=MESH,
        )
        copy.start()
        started.append(copy)

    def arrived_shared(k, slot):
        arrived(k, half * 3 + slot)

    def apply_wide(k):
        for part, m in ((0, 1), (1, 2)):
            hi, lo = halves(gath[k, m, col])
            vh[:, part * c : (part + 1) * c] = hi
            vl[:, part * c : (part + 1) * c] = lo

        def times(rows, hi, lo):
            return mm(dh[k % 2, rows, :], hi) + mm(dh[k % 2, rows, :], lo) + mm(dl[k % 2, rows, :], hi)

        def base(rows):
            return jnp.concatenate([gath[k, 1, col, rows, :], gath[k, 2, col, rows, :]], axis=1)

        for rows in tiles:
            x = 2.0 * base(rows) - times(rows, vh[...], vl[...])
            xh[rows, :], xl[rows, :] = halves(x)
        for rows in tiles:
            w = 2.0 * base(rows) - times(rows, xh[...], xl[...])
            w_ref[rows, :] = w
            vh[rows, :], vl[rows, :] = halves(w)
        for rows in tiles:
            out = 2.0 * w_ref[rows, :] - times(rows, vh[...], vl[...])
            sent[k, 0, rows, :] = out[:, :c]
            sent[k, 1, rows, :] = out[:, c:]

    def narrow(rows, ah, al, pair):
        both = mm(ah[rows, :], pair)
        return both[:, :c] + both[:, c:] + mm(al[rows, :], pair[:, :c])

    def put_pair(ref, rows, x):
        ref[rows, :c], ref[rows, c:] = halves(x)

    def apply_narrow(k, v_ref, write):
        put_pair(vh, slice(None), v_ref[...])
        for rows in tiles:
            put_pair(xh, rows, 2.0 * v_ref[rows, :] - narrow(rows, dh.at[k % 2], dl.at[k % 2], vh[...]))
        for rows in tiles:
            w = 2.0 * v_ref[rows, :] - narrow(rows, dh.at[k % 2], dl.at[k % 2], xh[...])
            w_ref[rows, :c] = w
            put_pair(vh, rows, w)
        for rows in tiles:
            write(rows, 2.0 * w_ref[rows, :c] - narrow(rows, dh.at[k % 2], dl.at[k % 2], vh[...]))

    def combined(k, first, second, old, write):
        p = k % 2
        put_pair(rh, slice(0, n), got[k, first])
        put_pair(rh, slice(n, 2 * n), got[k, second])
        for rows in tiles:
            pair = rh[...]
            both = mm(luh[p, rows, :], pair)
            value = both[:, :c] + both[:, c:] + mm(lul[p, rows, :], pair[:, :c])
            write(rows, old[rows, :] - value)

    def single(k, which, side, write):
        p = k % 2
        put_pair(rh, slice(0, n), got[k, which])
        cols = slice(side * n, (side + 1) * n)
        for rows in tiles:
            pair = rh[0:n, :]
            both = mm(luh[p, rows, cols], pair)
            value = both[:, :c] + both[:, c:] + mm(lul[p, rows, cols], pair[:, :c])
            write(rows, -value)

    def store(ref):
        def write(rows, value):
            ref[rows, :] = value

        return write

    def pack():
        live = lax.broadcasted_iota(jnp.int32, (1, entries), 1) < cnt_ref[...]
        owner = jnp.where(live, own_ref[...], -1)
        named = jnp.where(lax.broadcasted_iota(jnp.int32, (cycle, entries), 0) == owner, 1.0, 0.0)
        earlier = jnp.where(
            lax.broadcasted_iota(jnp.int32, (entries, entries), 0)
            < lax.broadcasted_iota(jnp.int32, (entries, entries), 1), 1.0, 0.0
        ).astype(BF16)
        before = mm(named.astype(BF16), earlier)
        rank = jnp.sum(named * before, axis=0, keepdims=True).astype(jnp.int32)
        target = jnp.where(live, owner * slots + rank, -1)
        row = row_ref[...]
        place = lax.broadcasted_iota(jnp.int32, (128, entries), 0)
        marks = jnp.where(place == rank, row // slots, jnp.where(place == rank + slots, row % slots, 0))
        out_m[...] = lax.dot_general(
            named.astype(BF16), marks.astype(F32).astype(BF16), (((1,), (1,)), ((), ())),
            preferred_element_type=F32,
        )[:, None, :]
        put_pair(vh, slice(None), x_ref[...])
        part = 256
        for t in range(out_v.shape[0] // part):
            pick = jnp.where(
                lax.broadcasted_iota(jnp.int32, (part, entries), 0) + t * part == target, 1.0, 0.0
            ).astype(BF16)
            both = mm(pick, vh[...])
            out_v[t * part : (t + 1) * part, :] = both[:, :c] + both[:, c:]

    def block_of(ref, index):
        return ref.at[pl.ds(pl.multiple_of(index * slots, slots), slots), :]

    def deliver():
        pltpu.make_async_copy(out_m.at[blk], in_m.at[blk], ps.at[3]).start()

        @pl.when(odd == 0)
        def _():
            pltpu.make_async_copy(block_of(out_v, blk), block_of(in_v, blk), ps.at[1]).start()

        @pl.when(odd == 1)
        def _():
            pltpu.make_async_remote_copy(
                src_ref=block_of(out_v, blk), dst_ref=block_of(in_v, blk), send_sem=ps.at[4], recv_sem=ps.at[1],
                device_id=(blk, across), device_id_type=MESH,
            ).start()

        @pl.loop(1, cycle)
        def _(step):
            to = upper(step)
            pltpu.make_async_remote_copy(
                src_ref=out_m.at[to], dst_ref=in_m.at[blk], send_sem=ps.at[2], recv_sem=ps.at[3],
                device_id=(to, (az + 2 * ((to // RING) % 2)) % 4), device_id_type=MESH,
            ).start()
            pltpu.make_async_remote_copy(
                src_ref=block_of(out_v, to), dst_ref=block_of(in_v, blk), send_sem=ps.at[0], recv_sem=ps.at[1],
                device_id=(to, (az + 2 * ((to // RING) % 2)) % 4), device_id_type=MESH,
            ).start()

    def unpack():
        pltpu.make_async_copy(in_m, in_m, ps.at[3]).wait()
        pltpu.make_async_copy(in_v, in_v, ps.at[1]).wait()
        total = in_v.shape[0]
        lane = lax.broadcasted_iota(jnp.int32, (128, total), 0)
        slot = lax.broadcasted_iota(jnp.int32, (128, total), 1) % slots
        spread = jnp.where(slot == lane, float(slots), jnp.where(slot + slots == lane, 1.0, 0.0))
        wide = mm(in_m[:, 0, :].astype(BF16), spread.astype(BF16))
        mine = lax.broadcasted_iota(jnp.int32, (cycle, total), 1) // slots == lax.broadcasted_iota(
            jnp.int32, (cycle, total), 0
        )
        mark = jnp.sum(jnp.where(mine, wide, 0.0), axis=0, keepdims=True).astype(jnp.int32)
        put_pair(rh, slice(None), in_v[...])
        for rows in tiles:
            pick = jnp.where(
                lax.broadcasted_iota(jnp.int32, (tile, total), 0) + rows.start == mark, 1.0, 0.0
            ).astype(BF16)
            both = mm(pick, rh[...])
            bcur[0, rows, :] = swap[0, odd, rows, :] + both[:, :c] + both[:, c:]

    eye = (
        lax.broadcasted_iota(jnp.int32, (n, c), 0) == lax.broadcasted_iota(jnp.int32, (n, c), 1) + az * c
    ).astype(F32)
    gath[0, 0, az] = d_ref[...] + eye
    gath[0, 1, az] = l_ref[...] - coupling * eye
    gath[0, 2, az] = u_ref[...] - coupling * eye
    pack()
    pl.semaphore_wait(barrier, 2 * cycle)
    for m in range(3):
        gather_start(0, m)

    PM, QM, YM, PP, QP, YP = range(6)
    def drain(copies):
        for copy in copies:
            copy.wait_send()
        started[:] = [copy for copy in started if not any(copy is other for other in copies)]


    ahead = []

    def right_side(k):
        s = 2**k
        last = k == LEVELS - 1
        shared = s == RING // 2
        if k == 0:
            swap_finish(0)
            unpack()
        else:
            if s == RING:
                arrived_shared(k - 1, 2)
            else:
                arrived(k - 1, YM)
                arrived(k - 1, YP)
            combined(k - 1, YM, YP, bcur.at[(k - 1) % 2], store(bcur.at[k % 2]))
        if last:
            swap_start(1, bcur.at[k % 2])
        apply_narrow(k, bcur.at[k % 2], store(sent.at[k, 2]))
        if last:
            drain(ahead)
        if last:
            send_last(k)
        elif shared:
            send_shared(k, 2)
        else:
            send(k, YM, 2, at(upper(s)))
            send(k, YP, 2, at(lower(s)))

    for k in range(LEVELS):
        s = 2**k
        last = k == LEVELS - 1
        shared = s == RING // 2
        gather_finish(k, 0, dh.at[k % 2], dl.at[k % 2], 0, (lambda: pass_on(2, 2)) if s == RING else None)
        if k == 0:
            gather_finish(k, 1, luh.at[k % 2], lul.at[k % 2], 0)
            apply_narrow(k, gath.at[k, 1, col], store(sent.at[k, 0]))
            send(k, PP, 0, at(lower(s)))
            send(k, PM, 0, at(upper(s)))
            gather_finish(k, 2, luh.at[k % 2], lul.at[k % 2], n)
            apply_narrow(k, gath.at[k, 2, col], store(sent.at[k, 1]))
            send(k, QM, 1, at(upper(s)))
            send(k, QP, 1, at(lower(s)))
            swap_start(0, b_ref)
            deliver()
        else:
            apply_wide(k)
        if k == 0:
            pass
        elif shared:
            send_shared(k, half)
            send_shared(k, 1 - half)
        else:
            ahead[:] = [send(k, QM, 1, at(upper(s))), send(k, PP, 0, at(lower(s)))]
            if not last:
                send(k, PM, 0, at(upper(s)))
                send(k, QP, 1, at(lower(s)))
        if k == 1:
            right_side(0)
        if k > 0:
            gather_finish(k, 1, luh.at[k % 2], lul.at[k % 2], 0)
            gather_finish(k, 2, luh.at[k % 2], lul.at[k % 2], n)
        if last:
            right_side(k)
        if shared:
            pass_on(k, 1 - half)
            right_side(k)
            pass_on(k, half)
            arrived_shared(k, 1 - half)
            arrived_shared(k, half)
        else:
            arrived(k, QM)
            arrived(k, PP)
        combined(k, QM, PP, gath.at[k, 0, col], store(gath.at[k + 1, 0, col]))
        gather_start(k + 1, 0)
        if not last:
            if not shared:
                arrived(k, PM)
            single(k, PM, 0, store(gath.at[k + 1, 1, col]))
            gather_start(k + 1, 1)
            if not shared:
                arrived(k, QP)
            single(k, QP, 1, store(gath.at[k + 1, 2, col]))
            gather_start(k + 1, 2)
            if k > 0 and not shared:
                right_side(k)
    gather_finish(LEVELS, 0, dh.at[LEVELS % 2], dl.at[LEVELS % 2], 0, lambda: pass_last(LEVELS - 1))
    arrived(LEVELS - 1, 2 + 3 * odd)
    swap_finish(1)
    combined(LEVELS - 1, YM, YP, swap.at[1, odd], store(bcur.at[LEVELS % 2]))
    apply_narrow(LEVELS, bcur.at[LEVELS % 2], store(o_ref))
    for copy in started:
        copy.wait_send()
    rest = pl.ds(0, (cycle - 1) * slots)
    pltpu.make_async_copy(out_v.at[rest, :], out_v.at[rest, :], ps.at[0]).wait()

    @pl.when(odd == 1)
    def _():
        pltpu.make_async_copy(block_of(out_v, blk), block_of(in_v, blk), ps.at[4]).wait()

    rest = pl.ds(0, cycle - 1)
    pltpu.make_async_copy(out_m.at[rest], out_m.at[rest], ps.at[2]).wait()


def on_device(lower_part, diag_part, upper_part, right_side, extra, owners, rows_in, counts):
    n, c = diag_part.shape[1:]
    entries = extra.shape[0]
    cycle = lax.axis_size("blk")
    slots = 2 * entries // cycle
    vmem = pl.BlockSpec(memory_space=pltpu.VMEM)
    out = pl.pallas_call(
        kernel,
        name="levels",
        out_shape=jax.ShapeDtypeStruct((n, c), F32),
        in_specs=[vmem] * 8,
        out_specs=vmem,
        scratch_shapes=[
            pltpu.VMEM((LEVELS + 1, 3, 4, n, c), F32),
            pltpu.VMEM((LEVELS, 3, n, c), F32),
            pltpu.VMEM((LEVELS, 6, n, c), F32),
            pltpu.VMEM((2, n, n), BF16),
            pltpu.VMEM((2, n, n), BF16),
            pltpu.VMEM((2, n, 2 * n), BF16),
            pltpu.VMEM((2, n, 2 * n), BF16),
            pltpu.VMEM((n, 2 * c), BF16),
            pltpu.VMEM((n, 2 * c), BF16),
            pltpu.VMEM((n, 2 * c), BF16),
            pltpu.VMEM((n, 2 * c), BF16),
            pltpu.VMEM((n, 2 * c), F32),
            pltpu.VMEM((2 * n, 2 * c), BF16),
            pltpu.VMEM((2, n, c), F32),
            pltpu.VMEM((cycle * slots, c), F32),
            pltpu.VMEM((cycle, 1, 128), F32),
            pltpu.VMEM((cycle * slots, c), F32),
            pltpu.VMEM((cycle, 1, 128), F32),
            pltpu.VMEM((2, 2, n, c), F32),
            pltpu.SemaphoreType.DMA((LEVELS + 1, 3, 3)),
            pltpu.SemaphoreType.DMA((LEVELS + 1, 3, 3)),
            pltpu.SemaphoreType.DMA((LEVELS, 3, 2)),
            pltpu.SemaphoreType.DMA((LEVELS, 6)),
            pltpu.SemaphoreType.DMA((5,)),
            pltpu.SemaphoreType.DMA((2,)),
            pltpu.SemaphoreType.DMA((2,)),
        ],
        compiler_params=pltpu.CompilerParams(
            collective_id=0, has_side_effects=True, vmem_limit_bytes=56 * 2**20
        ),
    )(lower_part[0], diag_part[0], upper_part[0], right_side[0], extra,
      owners.reshape(1, entries), rows_in.reshape(1, entries), counts.reshape(1, 1))
    return out[None]


def solution(mesh):
    placed = (
        P("blk", None, "az"),
        P("blk", None, "az"),
        P("blk", None, "az"),
        P("blk", None, "az"),
        P("blk", "az"),
        P("blk", None),
        P("blk"),
        P("blk"),
    )
    return jax.shard_map(
        on_device, mesh=mesh, in_specs=placed, out_specs=P("blk", None, "az"), check_vma=False
    )
```

```python
import functools

import jax
import jax.numpy as jnp
from jax import lax
from jax.experimental import pallas as pl
from jax.experimental.pallas import tpu as pltpu
from jax.sharding import PartitionSpec as P

coupling = 0.42
MESH = pl.DeviceIdType.MESH
LEVELS = 4
RING = 8
F32, BF16 = jnp.float32, jnp.bfloat16


def halves(x):
    hi = x.astype(BF16)
    return hi, (x - hi.astype(F32)).astype(BF16)


def mm(a, b):
    return jnp.dot(a, b, preferred_element_type=F32)


def kernel(
    l_ref, d_ref, u_ref, b_ref, x_ref, own_ref, row_ref, cnt_ref, o_ref,
    gath, sent, got, dh, dl, luh, lul, vh, vl, xh, xl, w_ref, rh, bcur,
    out_v, out_m, in_v, in_m, swap, gs, gr, es, er, ps, ws, wr,
):
    n = d_ref.shape[0]
    c = d_ref.shape[1]
    tile = n // 2
    tiles = [pl.ds(t * tile, tile) for t in range(2)]
    blk = lax.axis_index("blk")
    az = lax.axis_index("az")
    cycle = lax.axis_size("blk")
    mate = (az // 2) * 2 + 1 - az % 2
    across = (az + 2) % 4
    odd = (blk // RING) % 2
    col = (az + 2 * odd) % 4

    def lower(s):
        return (blk - s + cycle) % cycle

    def upper(s):
        return (blk + s) % cycle

    def at(row):
        return (row, (col + 2 * ((row // RING) % 2)) % 4)

    entries = x_ref.shape[0]
    slots = out_v.shape[0] // cycle
    barrier = pltpu.get_barrier_semaphore()
    pl.semaphore_signal(barrier, inc=1, device_id=(blk, mate), device_id_type=MESH)
    pl.semaphore_signal(barrier, inc=1, device_id=(blk, across), device_id_type=MESH)

    @pl.loop(1, cycle)
    def _(step):
        to = upper(step)
        pl.semaphore_signal(barrier, inc=1, device_id=(to, az), device_id_type=MESH)
        pl.semaphore_signal(barrier, inc=1, device_id=(to, (az + 2) % 4), device_id_type=MESH)

    started = []

    def gather_copy(k, m, which, slot, device):
        return pltpu.make_async_remote_copy(
            src_ref=gath.at[k, m, slot], dst_ref=gath.at[k, m, slot],
            send_sem=gs.at[k, m, which], recv_sem=gr.at[k, m, which],
            device_id=device, device_id_type=MESH,
        )

    def gather_start(k, m):
        mine = az if k == 0 else col
        one = gather_copy(k, m, 0, mine, (blk, mate))
        two = gather_copy(k, m, 1, mine, (blk, across))
        two.start()
        one.start()
        started.extend([one, two])

    def gather_finish(k, m, into_h, into_l, base, between=None):
        mine = az if k == 0 else col
        beside = (mine // 2) * 2 + 1 - mine % 2

        def put(slot):
            where = pl.ds(pl.multiple_of(base + slot * c, c), c)
            hi, lo = halves(gath[k, m, slot])
            into_h[:, where] = hi
            into_l[:, where] = lo

        put(mine)
        gather_copy(k, m, 0, beside, (blk, mate)).wait_recv()
        put(beside)
        if between is not None:
            between()
        gather_copy(k, m, 1, (mine + 2) % 4, (blk, across)).wait_recv()
        three = gather_copy(k, m, 2, (mine + 2) % 4, (blk, mate))
        three.start()
        started.append(three)
        put((mine + 2) % 4)
        gather_copy(k, m, 2, (beside + 2) % 4, (blk, mate)).wait_recv()
        put((beside + 2) % 4)

    def swap_copy(which, src):
        return pltpu.make_async_remote_copy(
            src_ref=src, dst_ref=swap.at[which, 1], send_sem=ws.at[which], recv_sem=wr.at[which],
            device_id=(blk, across), device_id_type=MESH,
        )

    def swap_start(which, src):
        swap[which, 0] = src[...]

        @pl.when(odd == 1)
        def _():
            swap_copy(which, swap.at[which, 0]).start()

    def swap_finish(which):
        @pl.when(odd == 1)
        def _():
            swap_copy(which, swap.at[which, 0]).wait()

    def send(k, which, slot, target):
        copy = pltpu.make_async_remote_copy(
            src_ref=sent.at[k, slot], dst_ref=got.at[k, which],
            send_sem=es.at[k, slot, which // 3], recv_sem=er.at[k, which],
            device_id=target, device_id_type=MESH,
        )
        copy.start()
        started.append(copy)
        return copy

    def arrived(k, which):
        pltpu.make_async_remote_copy(
            src_ref=sent.at[k, 0], dst_ref=got.at[k, which],
            send_sem=er.at[k, which], recv_sem=er.at[k, which],
            device_id=(blk, az), device_id_type=MESH,
        ).wait_recv()

    half = (blk % RING) // (RING // 2)
    near = (blk // RING) * RING + (blk + RING // 2) % RING
    far = (blk + RING * (1 - 2 * half) + cycle) % cycle

    def send_shared(k, slot):
        copy = pltpu.make_async_remote_copy(
            src_ref=sent.at[k, slot], dst_ref=got.at[k, half * 3 + slot],
            send_sem=es.at[k, slot, 0], recv_sem=er.at[k, half * 3 + slot],
            device_id=at(near), device_id_type=MESH,
        )
        copy.start()
        started.append(copy)

    def pass_on(k, slot):
        direct = (1 - half) * 3 + slot
        arrived(k, direct)
        copy = pltpu.make_async_remote_copy(
            src_ref=got.at[k, direct], dst_ref=got.at[k, half * 3 + slot],
            send_sem=es.at[k, slot, 1], recv_sem=er.at[k, half * 3 + slot],
            device_id=at(far), device_id_type=MESH,
        )
        copy.start()
        started.append(copy)

    def send_last(k):
        copy = pltpu.make_async_remote_copy(
            src_ref=sent.at[k, 2], dst_ref=got.at[k, 2 + 3 * odd],
            send_sem=es.at[k, 2, 0], recv_sem=er.at[k, 2 + 3 * odd],
            device_id=((blk + RING * (1 - 2 * odd) + cycle) % cycle, col), device_id_type=MESH,
        )
        copy.start()
        started.append(copy)

    def pass_last(k):
        direct = 2 + 3 * (1 - odd)
        arrived(k, direct)
        copy = pltpu.make_async_remote_copy(
            src_ref=got.at[k, direct], dst_ref=got.at[k, 2 + 3 * odd],
            send_sem=es.at[k, 2, 1], recv_sem=er.at[k, 2 + 3 * odd],
            device_id=((blk + 2 * RING * (1 - 2 * odd) + cycle) % cycle, az), device_id_type=MESH,
        )
        copy.start()
        started.append(copy)

    def arrived_shared(k, slot):
        arrived(k, half * 3 + slot)

    def apply_wide(k):
        for part, m in ((0, 1), (1, 2)):
            hi, lo = halves(gath[k, m, col])
            vh[:, part * c : (part + 1) * c] = hi
            vl[:, part * c : (part + 1) * c] = lo

        def times(rows, hi, lo):
            return mm(dh[k % 2, rows, :], hi) + mm(dh[k % 2, rows, :], lo) + mm(dl[k % 2, rows, :], hi)

        def base(rows):
            return jnp.concatenate([gath[k, 1, col, rows, :], gath[k, 2, col, rows, :]], axis=1)

        for rows in tiles:
            x = 2.0 * base(rows) - times(rows, vh[...], vl[...])
            xh[rows, :], xl[rows, :] = halves(x)
        for rows in tiles:
            w = 2.0 * base(rows) - times(rows, xh[...], xl[...])
            w_ref[rows, :] = w
            vh[rows, :], vl[rows, :] = halves(w)
        for rows in tiles:
            out = 2.0 * w_ref[rows, :] - times(rows, vh[...], vl[...])
            sent[k, 0, rows, :] = out[:, :c]
            sent[k, 1, rows, :] = out[:, c:]

    def narrow(rows, ah, al, pair):
        both = mm(ah[rows, :], pair)
        return both[:, :c] + both[:, c:] + mm(al[rows, :], pair[:, :c])

    def put_pair(ref, rows, x):
        ref[rows, :c], ref[rows, c:] = halves(x)

    def apply_narrow(k, v_ref, write):
        put_pair(vh, slice(None), v_ref[...])
        for rows in tiles:
            put_pair(xh, rows, 2.0 * v_ref[rows, :] - narrow(rows, dh.at[k % 2], dl.at[k % 2], vh[...]))
        for rows in tiles:
            w = 2.0 * v_ref[rows, :] - narrow(rows, dh.at[k % 2], dl.at[k % 2], xh[...])
            w_ref[rows, :c] = w
            put_pair(vh, rows, w)
        for rows in tiles:
            write(rows, 2.0 * w_ref[rows, :c] - narrow(rows, dh.at[k % 2], dl.at[k % 2], vh[...]))

    def combined(k, first, second, old, write):
        p = k % 2
        put_pair(rh, slice(0, n), got[k, first])
        put_pair(rh, slice(n, 2 * n), got[k, second])
        for rows in tiles:
            pair = rh[...]
            both = mm(luh[p, rows, :], pair)
            value = both[:, :c] + both[:, c:] + mm(lul[p, rows, :], pair[:, :c])
            write(rows, old[rows, :] - value)

    def single(k, which, side, write):
        p = k % 2
        put_pair(rh, slice(0, n), got[k, which])
        cols = slice(side * n, (side + 1) * n)
        for rows in tiles:
            pair = rh[0:n, :]
            both = mm(luh[p, rows, cols], pair)
            value = both[:, :c] + both[:, c:] + mm(lul[p, rows, cols], pair[:, :c])
            write(rows, -value)

    def store(ref):
        def write(rows, value):
            ref[rows, :] = value

        return write

    def pack():
        live = lax.broadcasted_iota(jnp.int32, (1, entries), 1) < cnt_ref[...]
        owner = jnp.where(live, own_ref[...], -1)
        named = jnp.where(lax.broadcasted_iota(jnp.int32, (cycle, entries), 0) == owner, 1.0, 0.0)
        earlier = jnp.where(
            lax.broadcasted_iota(jnp.int32, (entries, entries), 0)
            < lax.broadcasted_iota(jnp.int32, (entries, entries), 1), 1.0, 0.0
        ).astype(BF16)
        before = mm(named.astype(BF16), earlier)
        rank = jnp.sum(named * before, axis=0, keepdims=True).astype(jnp.int32)
        target = jnp.where(live, owner * slots + rank, -1)
        row = row_ref[...]
        place = lax.broadcasted_iota(jnp.int32, (128, entries), 0)
        marks = jnp.where(place == rank, row // slots, jnp.where(place == rank + slots, row % slots, 0))
        out_m[...] = lax.dot_general(
            named.astype(BF16), marks.astype(F32).astype(BF16), (((1,), (1,)), ((), ())),
            preferred_element_type=F32,
        )[:, None, :]
        put_pair(vh, slice(None), x_ref[...])
        part = 256
        for t in range(out_v.shape[0] // part):
            pick = jnp.where(
                lax.broadcasted_iota(jnp.int32, (part, entries), 0) + t * part == target, 1.0, 0.0
            ).astype(BF16)
            both = mm(pick, vh[...])
            out_v[t * part : (t + 1) * part, :] = both[:, :c] + both[:, c:]

    def block_of(ref, index):
        return ref.at[pl.ds(pl.multiple_of(index * slots, slots), slots), :]

    def deliver():
        pltpu.make_async_copy(out_m.at[blk], in_m.at[blk], ps.at[3]).start()

        @pl.when(odd == 0)
        def _():
            pltpu.make_async_copy(block_of(out_v, blk), block_of(in_v, blk), ps.at[1]).start()

        @pl.when(odd == 1)
        def _():
            pltpu.make_async_remote_copy(
                src_ref=block_of(out_v, blk), dst_ref=block_of(in_v, blk), send_sem=ps.at[4], recv_sem=ps.at[1],
                device_id=(blk, across), device_id_type=MESH,
            ).start()

        @pl.loop(1, cycle)
        def _(step):
            to = upper(step)
            pltpu.make_async_remote_copy(
                src_ref=out_m.at[to], dst_ref=in_m.at[blk], send_sem=ps.at[2], recv_sem=ps.at[3],
                device_id=(to, (az + 2 * ((to // RING) % 2)) % 4), device_id_type=MESH,
            ).start()
            pltpu.make_async_remote_copy(
                src_ref=block_of(out_v, to), dst_ref=block_of(in_v, blk), send_sem=ps.at[0], recv_sem=ps.at[1],
                device_id=(to, (az + 2 * ((to // RING) % 2)) % 4), device_id_type=MESH,
            ).start()

    def unpack():
        pltpu.make_async_copy(in_m, in_m, ps.at[3]).wait()
        pltpu.make_async_copy(in_v, in_v, ps.at[1]).wait()
        total = in_v.shape[0]
        lane = lax.broadcasted_iota(jnp.int32, (128, total), 0)
        slot = lax.broadcasted_iota(jnp.int32, (128, total), 1) % slots
        spread = jnp.where(slot == lane, float(slots), jnp.where(slot + slots == lane, 1.0, 0.0))
        wide = mm(in_m[:, 0, :].astype(BF16), spread.astype(BF16))
        mine = lax.broadcasted_iota(jnp.int32, (cycle, total), 1) // slots == lax.broadcasted_iota(
            jnp.int32, (cycle, total), 0
        )
        mark = jnp.sum(jnp.where(mine, wide, 0.0), axis=0, keepdims=True).astype(jnp.int32)
        put_pair(rh, slice(None), in_v[...])
        for rows in tiles:
            pick = jnp.where(
                lax.broadcasted_iota(jnp.int32, (tile, total), 0) + rows.start == mark, 1.0, 0.0
            ).astype(BF16)
            both = mm(pick, rh[...])
            bcur[0, rows, :] = swap[0, odd, rows, :] + both[:, :c] + both[:, c:]

    eye = (
        lax.broadcasted_iota(jnp.int32, (n, c), 0) == lax.broadcasted_iota(jnp.int32, (n, c), 1) + az * c
    ).astype(F32)
    gath[0, 0, az] = d_ref[...] + eye
    gath[0, 1, az] = l_ref[...] - coupling * eye
    gath[0, 2, az] = u_ref[...] - coupling * eye
    pack()
    pl.semaphore_wait(barrier, 2 * cycle)
    for m in range(3):
        gather_start(0, m)
    swap_start(0, b_ref)

    PM, QM, YM, PP, QP, YP = range(6)
    def drain(copies):
        for copy in copies:
            copy.wait_send()
        started[:] = [copy for copy in started if not any(copy is other for other in copies)]


    ahead = []

    def right_side(k):
        s = 2**k
        last = k == LEVELS - 1
        shared = s == RING // 2
        if k == 0:
            swap_finish(0)
            unpack()
        else:
            if s == RING:
                arrived_shared(k - 1, 2)
            else:
                arrived(k - 1, YM)
                arrived(k - 1, YP)
            combined(k - 1, YM, YP, bcur.at[(k - 1) % 2], store(bcur.at[k % 2]))
        if last:
            swap_start(1, bcur.at[k % 2])
        apply_narrow(k, bcur.at[k % 2], store(sent.at[k, 2]))
        if last:
            drain(ahead)
        if last:
            send_last(k)
        elif shared:
            send_shared(k, 2)
        else:
            send(k, YM, 2, at(upper(s)))
            send(k, YP, 2, at(lower(s)))

    for k in range(LEVELS):
        s = 2**k
        last = k == LEVELS - 1
        shared = s == RING // 2
        gather_finish(k, 0, dh.at[k % 2], dl.at[k % 2], 0)
        if k == 0:
            gather_finish(k, 1, luh.at[k % 2], lul.at[k % 2], 0)
            apply_narrow(k, gath.at[k, 1, col], store(sent.at[k, 0]))
            send(k, PP, 0, at(lower(s)))
            send(k, PM, 0, at(upper(s)))
            gather_finish(k, 2, luh.at[k % 2], lul.at[k % 2], n)
            apply_narrow(k, gath.at[k, 2, col], store(sent.at[k, 1]))
            send(k, QM, 1, at(upper(s)))
            send(k, QP, 1, at(lower(s)))
            deliver()
        else:
            apply_wide(k)
        if k == 0:
            pass
        elif shared:
            send_shared(k, half)
            send_shared(k, 1 - half)
        else:
            ahead[:] = [send(k, QM, 1, at(upper(s))), send(k, PP, 0, at(lower(s)))]
            if not last:
                send(k, PM, 0, at(upper(s)))
                send(k, QP, 1, at(lower(s)))
        if k > 0:
            right_side(k - 1)
            gather_finish(k, 1, luh.at[k % 2], lul.at[k % 2], 0)
            gather_finish(k, 2, luh.at[k % 2], lul.at[k % 2], n)
        if s == RING:
            pass_on(k - 1, 2)
        if shared:
            pass_on(k, 1 - half)
            pass_on(k, half)
            arrived_shared(k, 1 - half)
            arrived_shared(k, half)
        else:
            arrived(k, QM)
            arrived(k, PP)
        combined(k, QM, PP, gath.at[k, 0, col], store(gath.at[k + 1, 0, col]))
        gather_start(k + 1, 0)
        if not last:
            if not shared:
                arrived(k, PM)
            single(k, PM, 0, store(gath.at[k + 1, 1, col]))
            gather_start(k + 1, 1)
            if not shared:
                arrived(k, QP)
            single(k, QP, 1, store(gath.at[k + 1, 2, col]))
            gather_start(k + 1, 2)
    right_side(LEVELS - 1)
    gather_finish(LEVELS, 0, dh.at[LEVELS % 2], dl.at[LEVELS % 2], 0)
    pass_last(LEVELS - 1)
    arrived(LEVELS - 1, 2 + 3 * odd)
    swap_finish(1)
    combined(LEVELS - 1, YM, YP, swap.at[1, odd], store(bcur.at[LEVELS % 2]))
    apply_narrow(LEVELS, bcur.at[LEVELS % 2], store(o_ref))
    for copy in started:
        copy.wait_send()
    rest = pl.ds(0, (cycle - 1) * slots)
    pltpu.make_async_copy(out_v.at[rest, :], out_v.at[rest, :], ps.at[0]).wait()

    @pl.when(odd == 1)
    def _():
        pltpu.make_async_copy(block_of(out_v, blk), block_of(in_v, blk), ps.at[4]).wait()

    rest = pl.ds(0, cycle - 1)
    pltpu.make_async_copy(out_m.at[rest], out_m.at[rest], ps.at[2]).wait()


def on_device(lower_part, diag_part, upper_part, right_side, extra, owners, rows_in, counts):
    n, c = diag_part.shape[1:]
    entries = extra.shape[0]
    cycle = lax.axis_size("blk")
    slots = 2 * entries // cycle
    vmem = pl.BlockSpec(memory_space=pltpu.VMEM)
    out = pl.pallas_call(
        kernel,
        name="levels",
        out_shape=jax.ShapeDtypeStruct((n, c), F32),
        in_specs=[vmem] * 8,
        out_specs=vmem,
        scratch_shapes=[
            pltpu.VMEM((LEVELS + 1, 3, 4, n, c), F32),
            pltpu.VMEM((LEVELS, 3, n, c), F32),
            pltpu.VMEM((LEVELS, 6, n, c), F32),
            pltpu.VMEM((2, n, n), BF16),
            pltpu.VMEM((2, n, n), BF16),
            pltpu.VMEM((2, n, 2 * n), BF16),
            pltpu.VMEM((2, n, 2 * n), BF16),
            pltpu.VMEM((n, 2 * c), BF16),
            pltpu.VMEM((n, 2 * c), BF16),
            pltpu.VMEM((n, 2 * c), BF16),
            pltpu.VMEM((n, 2 * c), BF16),
            pltpu.VMEM((n, 2 * c), F32),
            pltpu.VMEM((2 * n, 2 * c), BF16),
            pltpu.VMEM((2, n, c), F32),
            pltpu.VMEM((cycle * slots, c), F32),
            pltpu.VMEM((cycle, 1, 128), F32),
            pltpu.VMEM((cycle * slots, c), F32),
            pltpu.VMEM((cycle, 1, 128), F32),
            pltpu.VMEM((2, 2, n, c), F32),
            pltpu.SemaphoreType.DMA((LEVELS + 1, 3, 3)),
            pltpu.SemaphoreType.DMA((LEVELS + 1, 3, 3)),
            pltpu.SemaphoreType.DMA((LEVELS, 3, 2)),
            pltpu.SemaphoreType.DMA((LEVELS, 6)),
            pltpu.SemaphoreType.DMA((5,)),
            pltpu.SemaphoreType.DMA((2,)),
            pltpu.SemaphoreType.DMA((2,)),
        ],
        compiler_params=pltpu.CompilerParams(
            collective_id=0, has_side_effects=True, vmem_limit_bytes=56 * 2**20
        ),
    )(lower_part[0], diag_part[0], upper_part[0], right_side[0], extra,
      owners.reshape(1, entries), rows_in.reshape(1, entries), counts.reshape(1, 1))
    return out[None]


def solution(mesh):
    placed = (
        P("blk", None, "az"),
        P("blk", None, "az"),
        P("blk", None, "az"),
        P("blk", None, "az"),
        P("blk", "az"),
        P("blk", None),
        P("blk"),
        P("blk"),
    )
    return jax.shard_map(
        on_device, mesh=mesh, in_specs=placed, out_specs=P("blk", None, "az"), check_vma=False
    )
```

```python
import functools

import jax
import jax.numpy as jnp
from jax import lax
from jax.experimental import pallas as pl
from jax.experimental.pallas import tpu as pltpu
from jax.sharding import PartitionSpec as P

coupling = 0.42
MESH = pl.DeviceIdType.MESH
LEVELS = 4
RING = 8
F32, BF16 = jnp.float32, jnp.bfloat16


def halves(x):
    hi = x.astype(BF16)
    return hi, (x - hi.astype(F32)).astype(BF16)


def mm(a, b):
    return jnp.dot(a, b, preferred_element_type=F32)


def kernel(
    l_ref, d_ref, u_ref, b_ref, x_ref, own_ref, row_ref, cnt_ref, o_ref,
    gath, sent, got, dh, dl, luh, lul, vh, vl, xh, xl, w_ref, rh, bcur,
    out_v, out_m, in_v, in_m, swap, gs, gr, es, er, ps, ws, wr,
):
    n = d_ref.shape[0]
    c = d_ref.shape[1]
    tile = n // 2
    tiles = [pl.ds(t * tile, tile) for t in range(2)]
    blk = lax.axis_index("blk")
    az = lax.axis_index("az")
    cycle = lax.axis_size("blk")
    mate = (az // 2) * 2 + 1 - az % 2
    across = (az + 2) % 4
    odd = (blk // RING) % 2
    col = (az + 2 * odd) % 4

    def lower(s):
        return (blk - s + cycle) % cycle

    def upper(s):
        return (blk + s) % cycle

    def at(row):
        return (row, (col + 2 * ((row // RING) % 2)) % 4)

    entries = x_ref.shape[0]
    slots = out_v.shape[0] // cycle
    barrier = pltpu.get_barrier_semaphore()
    pl.semaphore_signal(barrier, inc=1, device_id=(blk, mate), device_id_type=MESH)
    pl.semaphore_signal(barrier, inc=1, device_id=(blk, across), device_id_type=MESH)

    @pl.loop(1, cycle)
    def _(step):
        to = upper(step)
        pl.semaphore_signal(barrier, inc=1, device_id=(to, az), device_id_type=MESH)
        pl.semaphore_signal(barrier, inc=1, device_id=(to, (az + 2) % 4), device_id_type=MESH)

    started = []

    def gather_copy(k, m, which, slot, device):
        return pltpu.make_async_remote_copy(
            src_ref=gath.at[k, m, slot], dst_ref=gath.at[k, m, slot],
            send_sem=gs.at[k, m, which], recv_sem=gr.at[k, m, which],
            device_id=device, device_id_type=MESH,
        )

    def gather_start(k, m):
        mine = az if k == 0 else col
        one = gather_copy(k, m, 0, mine, (blk, mate))
        two = gather_copy(k, m, 1, mine, (blk, across))
        two.start()
        one.start()
        started.extend([one, two])

    def gather_finish(k, m, into_h, into_l, base, between=None):
        mine = az if k == 0 else col
        beside = (mine // 2) * 2 + 1 - mine % 2

        def put(slot):
            where = pl.ds(pl.multiple_of(base + slot * c, c), c)
            hi, lo = halves(gath[k, m, slot])
            into_h[:, where] = hi
            into_l[:, where] = lo

        put(mine)
        gather_copy(k, m, 0, beside, (blk, mate)).wait_recv()
        put(beside)
        if between is not None:
            between()
        gather_copy(k, m, 1, (mine + 2) % 4, (blk, across)).wait_recv()
        three = gather_copy(k, m, 2, (mine + 2) % 4, (blk, mate))
        three.start()
        started.append(three)
        put((mine + 2) % 4)
        gather_copy(k, m, 2, (beside + 2) % 4, (blk, mate)).wait_recv()
        put((beside + 2) % 4)

    def swap_copy(which, src):
        return pltpu.make_async_remote_copy(
            src_ref=src, dst_ref=swap.at[which, 1], send_sem=ws.at[which], recv_sem=wr.at[which],
            device_id=(blk, across), device_id_type=MESH,
        )

    def swap_start(which, src):
        swap[which, 0] = src[...]

        @pl.when(odd == 1)
        def _():
            swap_copy(which, swap.at[which, 0]).start()

    def swap_finish(which):
        @pl.when(odd == 1)
        def _():
            swap_copy(which, swap.at[which, 0]).wait()

    def send(k, which, slot, target):
        copy = pltpu.make_async_remote_copy(
            src_ref=sent.at[k, slot], dst_ref=got.at[k, which],
            send_sem=es.at[k, slot, which // 3], recv_sem=er.at[k, which],
            device_id=target, device_id_type=MESH,
        )
        copy.start()
        started.append(copy)
        return copy

    def arrived(k, which):
        pltpu.make_async_remote_copy(
            src_ref=sent.at[k, 0], dst_ref=got.at[k, which],
            send_sem=er.at[k, which], recv_sem=er.at[k, which],
            device_id=(blk, az), device_id_type=MESH,
        ).wait_recv()

    half = (blk % RING) // (RING // 2)
    near = (blk // RING) * RING + (blk + RING // 2) % RING
    far = (blk + RING * (1 - 2 * half) + cycle) % cycle

    def send_shared(k, slot):
        copy = pltpu.make_async_remote_copy(
            src_ref=sent.at[k, slot], dst_ref=got.at[k, half * 3 + slot],
            send_sem=es.at[k, slot, 0], recv_sem=er.at[k, half * 3 + slot],
            device_id=at(near), device_id_type=MESH,
        )
        copy.start()
        started.append(copy)

    def pass_on(k, slot):
        direct = (1 - half) * 3 + slot
        arrived(k, direct)
        copy = pltpu.make_async_remote_copy(
            src_ref=got.at[k, direct], dst_ref=got.at[k, half * 3 + slot],
            send_sem=es.at[k, slot, 1], recv_sem=er.at[k, half * 3 + slot],
            device_id=at(far), device_id_type=MESH,
        )
        copy.start()
        started.append(copy)

    def send_last(k):
        copy = pltpu.make_async_remote_copy(
            src_ref=sent.at[k, 2], dst_ref=got.at[k, 2 + 3 * odd],
            send_sem=es.at[k, 2, 0], recv_sem=er.at[k, 2 + 3 * odd],
            device_id=((blk + RING * (1 - 2 * odd) + cycle) % cycle, col), device_id_type=MESH,
        )
        copy.start()
        started.append(copy)

    def pass_last(k):
        direct = 2 + 3 * (1 - odd)
        arrived(k, direct)
        copy = pltpu.make_async_remote_copy(
            src_ref=got.at[k, direct], dst_ref=got.at[k, 2 + 3 * odd],
            send_sem=es.at[k, 2, 1], recv_sem=er.at[k, 2 + 3 * odd],
            device_id=((blk + 2 * RING * (1 - 2 * odd) + cycle) % cycle, az), device_id_type=MESH,
        )
        copy.start()
        started.append(copy)

    def arrived_shared(k, slot):
        arrived(k, half * 3 + slot)

    def apply_wide(k):
        for part, m in ((0, 1), (1, 2)):
            hi, lo = halves(gath[k, m, col])
            vh[:, part * c : (part + 1) * c] = hi
            vl[:, part * c : (part + 1) * c] = lo

        def times(rows, hi, lo):
            return mm(dh[k % 2, rows, :], hi) + mm(dh[k % 2, rows, :], lo) + mm(dl[k % 2, rows, :], hi)

        def base(rows):
            return jnp.concatenate([gath[k, 1, col, rows, :], gath[k, 2, col, rows, :]], axis=1)

        for rows in tiles:
            x = 2.0 * base(rows) - times(rows, vh[...], vl[...])
            xh[rows, :], xl[rows, :] = halves(x)
        for rows in tiles:
            w = 2.0 * base(rows) - times(rows, xh[...], xl[...])
            w_ref[rows, :] = w
            vh[rows, :], vl[rows, :] = halves(w)
        for rows in tiles:
            out = 2.0 * w_ref[rows, :] - times(rows, vh[...], vl[...])
            sent[k, 0, rows, :] = out[:, :c]
            sent[k, 1, rows, :] = out[:, c:]

    def narrow(rows, ah, al, pair):
        both = mm(ah[rows, :], pair)
        return both[:, :c] + both[:, c:] + mm(al[rows, :], pair[:, :c])

    def put_pair(ref, rows, x):
        ref[rows, :c], ref[rows, c:] = halves(x)

    def apply_narrow(k, v_ref, write):
        put_pair(vh, slice(None), v_ref[...])
        for rows in tiles:
            put_pair(xh, rows, 2.0 * v_ref[rows, :] - narrow(rows, dh.at[k % 2], dl.at[k % 2], vh[...]))
        for rows in tiles:
            w = 2.0 * v_ref[rows, :] - narrow(rows, dh.at[k % 2], dl.at[k % 2], xh[...])
            w_ref[rows, :c] = w
            put_pair(vh, rows, w)
        for rows in tiles:
            write(rows, 2.0 * w_ref[rows, :c] - narrow(rows, dh.at[k % 2], dl.at[k % 2], vh[...]))

    def combined(k, first, second, old, write):
        p = k % 2
        put_pair(rh, slice(0, n), got[k, first])
        put_pair(rh, slice(n, 2 * n), got[k, second])
        for rows in tiles:
            pair = rh[...]
            both = mm(luh[p, rows, :], pair)
            value = both[:, :c] + both[:, c:] + mm(lul[p, rows, :], pair[:, :c])
            write(rows, old[rows, :] - value)

    def single(k, which, side, write):
        p = k % 2
        put_pair(rh, slice(0, n), got[k, which])
        cols = slice(side * n, (side + 1) * n)
        for rows in tiles:
            pair = rh[0:n, :]
            both = mm(luh[p, rows, cols], pair)
            value = both[:, :c] + both[:, c:] + mm(lul[p, rows, cols], pair[:, :c])
            write(rows, -value)

    def store(ref):
        def write(rows, value):
            ref[rows, :] = value

        return write

    def pack():
        live = lax.broadcasted_iota(jnp.int32, (1, entries), 1) < cnt_ref[...]
        owner = jnp.where(live, own_ref[...], -1)
        named = jnp.where(lax.broadcasted_iota(jnp.int32, (cycle, entries), 0) == owner, 1.0, 0.0)
        earlier = jnp.where(
            lax.broadcasted_iota(jnp.int32, (entries, entries), 0)
            < lax.broadcasted_iota(jnp.int32, (entries, entries), 1), 1.0, 0.0
        ).astype(BF16)
        before = mm(named.astype(BF16), earlier)
        rank = jnp.sum(named * before, axis=0, keepdims=True).astype(jnp.int32)
        target = jnp.where(live, owner * slots + rank, -1)
        row = row_ref[...]
        place = lax.broadcasted_iota(jnp.int32, (128, entries), 0)
        marks = jnp.where(place == rank, row // slots, jnp.where(place == rank + slots, row % slots, 0))
        out_m[...] = lax.dot_general(
            named.astype(BF16), marks.astype(F32).astype(BF16), (((1,), (1,)), ((), ())),
            preferred_element_type=F32,
        )[:, None, :]
        put_pair(vh, slice(None), x_ref[...])
        part = 256
        for t in range(out_v.shape[0] // part):
            pick = jnp.where(
                lax.broadcasted_iota(jnp.int32, (part, entries), 0) + t * part == target, 1.0, 0.0
            ).astype(BF16)
            both = mm(pick, vh[...])
            out_v[t * part : (t + 1) * part, :] = both[:, :c] + both[:, c:]

    def block_of(ref, index):
        return ref.at[pl.ds(pl.multiple_of(index * slots, slots), slots), :]

    def deliver():
        pltpu.make_async_copy(out_m.at[blk], in_m.at[blk], ps.at[3]).start()

        @pl.when(odd == 0)
        def _():
            pltpu.make_async_copy(block_of(out_v, blk), block_of(in_v, blk), ps.at[1]).start()

        @pl.when(odd == 1)
        def _():
            pltpu.make_async_remote_copy(
                src_ref=block_of(out_v, blk), dst_ref=block_of(in_v, blk), send_sem=ps.at[4], recv_sem=ps.at[1],
                device_id=(blk, across), device_id_type=MESH,
            ).start()

        @pl.loop(1, cycle)
        def _(step):
            to = upper(step)
            pltpu.make_async_remote_copy(
                src_ref=out_m.at[to], dst_ref=in_m.at[blk], send_sem=ps.at[2], recv_sem=ps.at[3],
                device_id=(to, (az + 2 * ((to // RING) % 2)) % 4), device_id_type=MESH,
            ).start()
            pltpu.make_async_remote_copy(
                src_ref=block_of(out_v, to), dst_ref=block_of(in_v, blk), send_sem=ps.at[0], recv_sem=ps.at[1],
                device_id=(to, (az + 2 * ((to // RING) % 2)) % 4), device_id_type=MESH,
            ).start()

    def unpack():
        pltpu.make_async_copy(in_m, in_m, ps.at[3]).wait()
        pltpu.make_async_copy(in_v, in_v, ps.at[1]).wait()
        total = in_v.shape[0]
        lane = lax.broadcasted_iota(jnp.int32, (128, total), 0)
        slot = lax.broadcasted_iota(jnp.int32, (128, total), 1) % slots
        spread = jnp.where(slot == lane, float(slots), jnp.where(slot + slots == lane, 1.0, 0.0))
        wide = mm(in_m[:, 0, :].astype(BF16), spread.astype(BF16))
        mine = lax.broadcasted_iota(jnp.int32, (cycle, total), 1) // slots == lax.broadcasted_iota(
            jnp.int32, (cycle, total), 0
        )
        mark = jnp.sum(jnp.where(mine, wide, 0.0), axis=0, keepdims=True).astype(jnp.int32)
        put_pair(rh, slice(None), in_v[...])
        for rows in tiles:
            pick = jnp.where(
                lax.broadcasted_iota(jnp.int32, (tile, total), 0) + rows.start == mark, 1.0, 0.0
            ).astype(BF16)
            both = mm(pick, rh[...])
            bcur[0, rows, :] = swap[0, odd, rows, :] + both[:, :c] + both[:, c:]

    eye = (
        lax.broadcasted_iota(jnp.int32, (n, c), 0) == lax.broadcasted_iota(jnp.int32, (n, c), 1) + az * c
    ).astype(F32)
    gath[0, 0, az] = d_ref[...] + eye
    gath[0, 1, az] = l_ref[...] - coupling * eye
    gath[0, 2, az] = u_ref[...] - coupling * eye
    pack()
    pl.semaphore_wait(barrier, 2 * cycle)
    for m in range(3):
        gather_start(0, m)
    swap_start(0, b_ref)

    PM, QM, YM, PP, QP, YP = range(6)
    def drain(copies):
        for copy in copies:
            copy.wait_send()
        started[:] = [copy for copy in started if not any(copy is other for other in copies)]


    ahead = []

    def right_side(k):
        s = 2**k
        last = k == LEVELS - 1
        shared = s == RING // 2
        if k == 0:
            swap_finish(0)
            unpack()
        else:
            if s == RING:
                arrived_shared(k - 1, 2)
            else:
                arrived(k - 1, YM)
                arrived(k - 1, YP)
            combined(k - 1, YM, YP, bcur.at[(k - 1) % 2], store(bcur.at[k % 2]))
        if last:
            swap_start(1, bcur.at[k % 2])
        apply_narrow(k, bcur.at[k % 2], store(sent.at[k, 2]))
        if last:
            drain(ahead)
        if last:
            send_last(k)
        elif shared:
            send_shared(k, 2)
        else:
            send(k, YM, 2, at(upper(s)))
            send(k, YP, 2, at(lower(s)))

    for k in range(LEVELS):
        s = 2**k
        last = k == LEVELS - 1
        shared = s == RING // 2
        gather_finish(k, 0, dh.at[k % 2], dl.at[k % 2], 0)
        if k == 0:
            gather_finish(k, 1, luh.at[k % 2], lul.at[k % 2], 0)
            apply_narrow(k, gath.at[k, 1, col], store(sent.at[k, 0]))
            send(k, PP, 0, at(lower(s)))
            send(k, PM, 0, at(upper(s)))
            gather_finish(k, 2, luh.at[k % 2], lul.at[k % 2], n)
            apply_narrow(k, gath.at[k, 2, col], store(sent.at[k, 1]))
            send(k, QM, 1, at(upper(s)))
            send(k, QP, 1, at(lower(s)))
            deliver()
        else:
            apply_wide(k)
        if k == 0:
            pass
        elif shared:
            send_shared(k, half)
            send_shared(k, 1 - half)
        else:
            ahead[:] = [send(k, QM, 1, at(upper(s))), send(k, PP, 0, at(lower(s)))]
            if not last:
                send(k, PM, 0, at(upper(s)))
                send(k, QP, 1, at(lower(s)))
        if k > 0:
            if not last:
                right_side(k - 1)
            gather_finish(k, 1, luh.at[k % 2], lul.at[k % 2], 0)
            gather_finish(k, 2, luh.at[k % 2], lul.at[k % 2], n)
        if s == RING:
            pass_on(k - 1, 2)
        if shared:
            pass_on(k, 1 - half)
            pass_on(k, half)
            arrived_shared(k, 1 - half)
            arrived_shared(k, half)
        else:
            arrived(k, QM)
            arrived(k, PP)
        combined(k, QM, PP, gath.at[k, 0, col], store(gath.at[k + 1, 0, col]))
        gather_start(k + 1, 0)
        if not last:
            if not shared:
                arrived(k, PM)
            single(k, PM, 0, store(gath.at[k + 1, 1, col]))
            gather_start(k + 1, 1)
            if not shared:
                arrived(k, QP)
            single(k, QP, 1, store(gath.at[k + 1, 2, col]))
            gather_start(k + 1, 2)
            if shared:
                right_side(k)
    right_side(LEVELS - 1)
    gather_finish(LEVELS, 0, dh.at[LEVELS % 2], dl.at[LEVELS % 2], 0)
    pass_last(LEVELS - 1)
    arrived(LEVELS - 1, 2 + 3 * odd)
    swap_finish(1)
    combined(LEVELS - 1, YM, YP, swap.at[1, odd], store(bcur.at[LEVELS % 2]))
    apply_narrow(LEVELS, bcur.at[LEVELS % 2], store(o_ref))
    for copy in started:
        copy.wait_send()
    rest = pl.ds(0, (cycle - 1) * slots)
    pltpu.make_async_copy(out_v.at[rest, :], out_v.at[rest, :], ps.at[0]).wait()

    @pl.when(odd == 1)
    def _():
        pltpu.make_async_copy(block_of(out_v, blk), block_of(in_v, blk), ps.at[4]).wait()

    rest = pl.ds(0, cycle - 1)
    pltpu.make_async_copy(out_m.at[rest], out_m.at[rest], ps.at[2]).wait()


def on_device(lower_part, diag_part, upper_part, right_side, extra, owners, rows_in, counts):
    n, c = diag_part.shape[1:]
    entries = extra.shape[0]
    cycle = lax.axis_size("blk")
    slots = 2 * entries // cycle
    vmem = pl.BlockSpec(memory_space=pltpu.VMEM)
    out = pl.pallas_call(
        kernel,
        name="levels",
        out_shape=jax.ShapeDtypeStruct((n, c), F32),
        in_specs=[vmem] * 8,
        out_specs=vmem,
        scratch_shapes=[
            pltpu.VMEM((LEVELS + 1, 3, 4, n, c), F32),
            pltpu.VMEM((LEVELS, 3, n, c), F32),
            pltpu.VMEM((LEVELS, 6, n, c), F32),
            pltpu.VMEM((2, n, n), BF16),
            pltpu.VMEM((2, n, n), BF16),
            pltpu.VMEM((2, n, 2 * n), BF16),
            pltpu.VMEM((2, n, 2 * n), BF16),
            pltpu.VMEM((n, 2 * c), BF16),
            pltpu.VMEM((n, 2 * c), BF16),
            pltpu.VMEM((n, 2 * c), BF16),
            pltpu.VMEM((n, 2 * c), BF16),
            pltpu.VMEM((n, 2 * c), F32),
            pltpu.VMEM((2 * n, 2 * c), BF16),
            pltpu.VMEM((2, n, c), F32),
            pltpu.VMEM((cycle * slots, c), F32),
            pltpu.VMEM((cycle, 1, 128), F32),
            pltpu.VMEM((cycle * slots, c), F32),
            pltpu.VMEM((cycle, 1, 128), F32),
            pltpu.VMEM((2, 2, n, c), F32),
            pltpu.SemaphoreType.DMA((LEVELS + 1, 3, 3)),
            pltpu.SemaphoreType.DMA((LEVELS + 1, 3, 3)),
            pltpu.SemaphoreType.DMA((LEVELS, 3, 2)),
            pltpu.SemaphoreType.DMA((LEVELS, 6)),
            pltpu.SemaphoreType.DMA((5,)),
            pltpu.SemaphoreType.DMA((2,)),
            pltpu.SemaphoreType.DMA((2,)),
        ],
        compiler_params=pltpu.CompilerParams(
            collective_id=0, has_side_effects=True, vmem_limit_bytes=56 * 2**20
        ),
    )(lower_part[0], diag_part[0], upper_part[0], right_side[0], extra,
      owners.reshape(1, entries), rows_in.reshape(1, entries), counts.reshape(1, 1))
    return out[None]


def solution(mesh):
    placed = (
        P("blk", None, "az"),
        P("blk", None, "az"),
        P("blk", None, "az"),
        P("blk", None, "az"),
        P("blk", "az"),
        P("blk", None),
        P("blk"),
        P("blk"),
    )
    return jax.shard_map(
        on_device, mesh=mesh, in_specs=placed, out_specs=P("blk", None, "az"), check_vma=False
    )
```
